32 devices in a mesh: case: 2 (over y), phase: 4 (over x, core), slab: 4 (over z).
Axes of the slice: x: 2, y: 2, z: 4, core: 2. Of those that a mesh axis runs over, the one named last changes fastest.
Arguments:
- fine_images: float32 [8, 64, 128, 512], P(('case', 'phase'), 'slab'), parts along dimension 0, may hold values from -6 to 6
- offsets: int32 [8, 3, 32, 64, 256], P(('case', 'phase'), None, 'slab'), parts along dimension 0, may hold values from -4 to 4
- velocity_init: float32 [8, 3, 32, 64, 256], P(('case', 'phase'), None, 'slab'), parts along dimension 0, may hold values from -3 to 3
Outputs:
- velocity: float32 [8, 3, 32, 64, 256], P(('case', 'phase'), None, 'slab'), parts along dimension 0
The draws below stay inside these ranges and needn't reach their ends.
There are 2 independent parts, one for each index of `case`. The reference program is written for one: setup_inputs(seed, part) draws one part's arguments, and reference() takes and returns one part's arrays. A program takes and returns all parts, laid end to end along the dimension named above; each array names one. Nothing has to cross between parts.
All inputs are finite; a program needn't handle non-finite values.
Results may differ from the reference program's by a relative error of at most 0.000076.
Values sent between devices are 32-bit elements; how exact they have to be, the bound alone decides.
No kernel may reach another device: no remote copies, remote signals or barrier semaphores. Data moves between devices by JAX's collectives and lax.ppermute only.
A program may use at most 64 MiB of HBM per device.

```python
import jax
import jax.numpy as jnp
from jax import lax

NX = 512
NY = 128
ITERS = 2
PHASES = 4
NZ = 64
CZ = 32
CY = 64
CX = 256


def with_ends(drawn, key, smallest, high):
    index_at = [jax.random.randint(jax.random.fold_in(key, axis), (), 0, length) for axis, length in enumerate(drawn.shape)]
    main_axis = drawn.shape.index(max(drawn.shape))
    beside = index_at[:main_axis] + [(index_at[main_axis] + 1) % drawn.shape[main_axis]] + index_at[main_axis + 1:]
    return drawn.at[tuple(index_at)].set(smallest).at[tuple(beside)].set(high)


def block_levels(key, shape, cuts, least, top_value):
    level = 1.0
    for position, blocks in cuts:
        heights = jax.random.uniform(jax.random.fold_in(jax.random.fold_in(key, 6), position), (blocks,), jnp.float32, least / len(cuts), top_value / len(cuts))
        level = level * jnp.repeat(jnp.exp(heights), shape[position] // blocks).reshape((-1,) + (1,) * (len(shape) - 1 - position))
    return level


def centred(rng, shape, spread, bound, shards=(), kind=jnp.bfloat16):
    entries = spread * jax.random.normal(rng, shape, jnp.float32)
    if shards:
        entries = entries * block_levels(rng, shape, shards, -0.22, 0.18)
    return jnp.clip(entries, -bound, bound).astype(kind)


def setup_inputs(seed: int = 0, part: int = 0) -> dict:
    arg_keys = jax.random.split(jax.random.key(seed), 4)
    part_splits = jax.random.split(jax.random.fold_in(arg_keys[3], part), 4)
    fine_images = centred(part_splits[0], (PHASES, NZ, NY, NX), 1.0, 6.0, ((0, 4), (1, 4)), jnp.float32)
    offsets = with_ends(jax.random.randint(part_splits[1], (PHASES, 3, CZ, CY, CX), -4, 5), jax.random.fold_in(part_splits[1], 1), -4, 4).astype(jnp.int32)
    velocity_init = centred(part_splits[2], (PHASES, 3, CZ, CY, CX), 0.5, 3.0, ((0, 4), (2, 4)), jnp.float32)
    return dict(fine_images=fine_images, offsets=offsets, velocity_init=velocity_init)


def pad_axis(values, dimension, width):
    widths = [(0, 0)] * values.ndim
    widths[dimension] = (width, width)
    return jnp.pad(values, widths)


def halve_axis(values, dimension):
    length = values.shape[dimension] - 2
    pieces = [lax.slice_in_dim(values, offset, offset + length - 1, stride=2, axis=dimension) for offset in range(4)]
    return (pieces[0] + 3.0 * pieces[1] + 3.0 * pieces[2] + pieces[3]) * 0.125


def gradient_axis(values, dimension):
    length = values.shape[dimension] - 2
    upper = lax.slice_in_dim(values, 2, 2 + length, axis=dimension)
    lower = lax.slice_in_dim(values, 0, length, axis=dimension)
    return (upper - lower) * 0.5


def smooth_axis(values, dimension):
    length = values.shape[dimension] - 2
    lower = lax.slice_in_dim(values, 0, length, axis=dimension)
    middle = lax.slice_in_dim(values, 1, 1 + length, axis=dimension)
    upper = lax.slice_in_dim(values, 2, 2 + length, axis=dimension)
    return (lower + 2.0 * middle + upper) * 0.25


def axis_weights(offsets):
    return [jnp.where(2 * displace == offsets, 1.0, jnp.where(jnp.abs(2 * displace - offsets) == 1, 0.5, 0.0)).astype(jnp.float32) for displace in range(-2, 3)]


def warp_moving(moving_padded, offsets):
    layers, height, breadth = offsets.shape[2], offsets.shape[3], offsets.shape[4]
    weights_z = axis_weights(offsets[:, 0])
    weights_y = axis_weights(offsets[:, 1])
    weights_x = axis_weights(offsets[:, 2])
    shape = offsets[:, 0].shape
    warped = jnp.zeros(shape, jnp.float32)
    for index_z in range(5):
        plane_sum = jnp.zeros(shape, jnp.float32)
        for index_y in range(5):
            line_sum = jnp.zeros(shape, jnp.float32)
            for index_x in range(5):
                window = moving_padded[:, index_z:index_z + layers, index_y:index_y + height, index_x:index_x + breadth]
                line_sum = line_sum + weights_x[index_x] * window
            plane_sum = plane_sum + weights_y[index_y] * line_sum
        warped = warped + weights_z[index_z] * plane_sum
    return warped


def reference(fine_images, offsets, velocity_init):
    coarse = halve_axis(pad_axis(fine_images, 1, 1), 1)
    coarse = halve_axis(pad_axis(coarse, 2, 1), 2)
    coarse = halve_axis(pad_axis(coarse, 3, 1), 3)
    target = jnp.roll(coarse, -1, axis=0)
    grad_z = gradient_axis(pad_axis(target, 1, 1), 1)
    grad_y = gradient_axis(pad_axis(target, 2, 1), 2)
    grad_x = gradient_axis(pad_axis(target, 3, 1), 3)
    gradients = jnp.stack([grad_z, grad_y, grad_x], axis=1)
    norm_squared = grad_z * grad_z + grad_y * grad_y + grad_x * grad_x
    moving_padded = pad_axis(pad_axis(pad_axis(coarse, 1, 2), 2, 2), 3, 2)
    warped_base = warp_moving(moving_padded, offsets)
    velocity = velocity_init
    for iteration in range(ITERS):
        warped = warped_base + velocity[:, 0] * grad_z + velocity[:, 1] * grad_y + velocity[:, 2] * grad_x
        mismatch = warped - target
        denominator = norm_squared + mismatch * mismatch + 1.0
        velocity = velocity - (mismatch / denominator)[:, None] * gradients
        velocity = smooth_axis(pad_axis(velocity, 2, 1), 2)
        velocity = smooth_axis(pad_axis(velocity, 3, 1), 3)
        velocity = smooth_axis(pad_axis(velocity, 4, 1), 4)
        velocity = (jnp.roll(velocity, 1, axis=0) + 2.0 * velocity + jnp.roll(velocity, -1, axis=0)) * 0.25
    return velocity
```

```python
import functools

import jax
import jax.numpy as jnp
from jax import lax
from jax.experimental import pallas as pl
from jax.experimental.pallas import tpu as pltpu
from jax.sharding import PartitionSpec as P

ITERS = 2
RIM = 8
F32 = jnp.float32
BF16 = jnp.bfloat16


def launch(body, outs, ins, scratch=(), anys=(), grid=None, in_specs=None, out_specs=None, flops=0):
    vmem = pl.BlockSpec(memory_space=pltpu.VMEM)
    anym = pl.BlockSpec(memory_space=pl.ANY)
    if in_specs is None:
        in_specs = [anym if i in anys else vmem for i in range(len(ins))]
    if out_specs is None:
        out_specs = [vmem for _ in outs]
    moved = sum(4 * x.size for x in ins) + sum(4 * o.size for o in outs)
    params = dict(grid=grid) if grid is not None else {}
    return pl.pallas_call(
        body,
        out_shape=outs,
        in_specs=in_specs,
        out_specs=out_specs,
        scratch_shapes=scratch,
        compiler_params=pltpu.CompilerParams(vmem_limit_bytes=48 * 2**20),
        cost_estimate=pl.CostEstimate(flops=flops, bytes_accessed=moved, transcendentals=0),
        **params,
    )(*ins)


def shape(*dims):
    return jax.ShapeDtypeStruct(dims, F32)


def chip_and_core():
    phase = lax.axis_index("phase")
    return phase // 2, phase % 2


def slab_place():
    slab = lax.axis_index("slab")
    last = lax.axis_size("slab") - 1
    return slab % 2, slab > 0, slab < last


def shift_rows(a, up):
    zero = jnp.zeros((1, a.shape[1]), a.dtype)
    return jnp.concatenate([a[1:], zero], 0) if up else jnp.concatenate([zero, a[:-1]], 0)


def shift_lanes(a, step):
    width = a.shape[1]
    lane = lax.broadcasted_iota(jnp.int32, a.shape, 1)
    moved = pltpu.roll(a, (-step) % width, 1)
    keep = lane < width - step if step > 0 else lane >= -step
    return jnp.where(keep, moved, 0.0)


def halve_kernel(fine, part, edge, buf_a, buf_b, mat, rows, prev):
    k = pl.program_id(0)
    last = pl.num_programs(0) - 1
    deep, tall, wide = fine.shape

    @pl.when(k == 0)
    def _():
        i = lax.broadcasted_iota(jnp.int32, mat.shape, 0)
        j = lax.broadcasted_iota(jnp.int32, mat.shape, 1)
        d = i - 2 * j
        inner = (d == 0) | (d == 1)
        outer = (d == -1) | (d == 2)
        mat[...] = jnp.where(inner, 0.375, jnp.where(outer, 0.125, 0.0)).astype(BF16)

    f = fine[...].reshape(deep * tall, wide)
    hi = f.astype(BF16)
    lo = (f - hi.astype(F32)).astype(BF16)
    w = mat[...]
    got = jnp.dot(hi, w, preferred_element_type=F32) + jnp.dot(lo, w, preferred_element_type=F32)
    half = tall // 2
    cut = rows.shape[2]
    for c in range(rows.shape[0]):
        rows[c] = got[:, c * cut : (c + 1) * cut]
    layers = []
    for z in range(deep):
        cols = []
        for c in range(rows.shape[0]):
            even = rows[c, pl.ds(z * tall, half, 2), :]
            odd = rows[c, pl.ds(z * tall + 1, half, 2), :]
            cols.append(
                (shift_rows(odd, False) + shift_rows(even, True) + 3.0 * (even + odd)) * (1.0 / 64.0)
            )
        layers.append(jnp.concatenate(cols, 1))
    even, odd = layers
    mid = 3.0 * (even + odd)

    @pl.when(k == 0)
    def _():
        edge[0] = even
        part[0] = mid

    @pl.when(k > 0)
    def _():
        part[k] = mid + prev[...]
        part[k - 1] += even

    prev[...] = odd

    @pl.when(k == last)
    def _():
        edge[1] = odd
        parity, _, _ = slab_place()
        n = part.shape[0]
        for i in range(4):
            above = odd if i == 3 else part[n - 3 + i]
            below = edge[0] if i == 0 else part[i - 1]
            buf_a[i] = jnp.where(parity == 0, above, below)
            buf_b[i] = jnp.where(parity == 0, below, above)


def join_kernel(part, edge, got_a, got_b, ext, near, far):
    n = part.shape[0]
    parity, has_below, has_above = slab_place()
    x, _ = chip_and_core()
    for i in range(3):
        low = jnp.where(parity == 0, got_b[i], got_a[i])
        high = jnp.where(parity == 0, got_a[i + 1], got_b[i + 1])
        if i == 2:
            low = jnp.where(has_below, low + edge[0], 0.0)
        if i == 0:
            high = jnp.where(has_above, high + edge[1], 0.0)
        ext[i] = low
        ext[n + 3 + i] = high
    for i in range(n):
        v = part[i]
        if i == 0:
            v = v + jnp.where(parity == 0, got_b[3], got_a[3])
        if i == n - 1:
            v = v + jnp.where(parity == 0, got_a[0], got_b[0])
        ext[i + 3] = v
    span = near.shape[1]
    step = ext.shape[1] - span
    near[...] = ext[:, pl.ds(pl.multiple_of(x * step, 8), span), :]
    far[...] = ext[:, pl.ds(pl.multiple_of((1 - x) * step, 8), span), :]


def warp_kernel(ext, offs, near, far, wide, full):
    n, tall = offs.shape[1], ext.shape[1]
    depth = n + 4
    columns, lanes = wide.shape[1], wide.shape[4]
    blank = jnp.zeros((8, lanes), F32)

    def fill(z, carry):
        v = ext[z + 1]
        for s in range(5):
            moved = v if s == 2 else shift_lanes(v, s - 2)
            for c in range(columns):
                wide[s, c, z, pl.ds(0, 8), :] = blank
                wide[s, c, z, pl.ds(8, tall), :] = moved[:, c * lanes : (c + 1) * lanes]
                wide[s, c, z, pl.ds(8 + tall, 8), :] = blank
        return carry

    lax.fori_loop(0, depth, fill, 0)

    def weights(comp, z, y, c):
        h = offs[comp, z, pl.ds(y, 8), pl.ds(c * lanes, lanes)].astype(F32) * 0.5
        return [jnp.maximum(1.0 - jnp.abs(h - (s - 2.0)), 0.0) for s in range(5)]

    def tile(i, carry):
        z = i // (tall // 8)
        y = pl.multiple_of((i % (tall // 8)) * 8, 8)
        for c in range(columns):
            wz, wy, wx = (weights(m, z, y, c) for m in range(3))
            total = None
            for a in range(5):
                plane = None
                for b in range(5):
                    line = None
                    for s in range(5):
                        term = wx[s] * wide[s, c, z + a, pl.ds(y + 6 + b, 8), :]
                        line = term if line is None else line + term
                    line = wy[b] * line
                    plane = line if plane is None else plane + line
                plane = wz[a] * plane
                total = plane if total is None else total + plane
            full[z, pl.ds(y, 8), pl.ds(c * lanes, lanes)] = total
        return carry

    lax.fori_loop(0, n * (tall // 8), tile, 0)
    x, _ = chip_and_core()
    span = near.shape[1]
    step = tall - span
    near[...] = full[:, pl.ds(pl.multiple_of(x * step, 8), span), :]
    far[...] = full[:, pl.ds(pl.multiple_of((1 - x) * step, 8), span), :]


def cut_kernel(vel, far, sem):
    x, _ = chip_and_core()
    span = far.shape[2]
    step = vel.shape[2] - span
    copy = pltpu.make_async_copy(
        vel.at[:, :, pl.ds(pl.multiple_of((1 - x) * step, 8), span), :], far, sem
    )
    copy.start()
    copy.wait()


def rim_velocity_kernel(vel, other, buf_a, buf_b, stage, sem):
    x, _ = chip_and_core()
    parity, _, _ = slab_place()
    n = vel.shape[1]
    span = other.shape[2]
    start = pl.multiple_of(x * (vel.shape[2] - span), 8)
    copies = [
        pltpu.make_async_copy(vel.at[:, pl.ds(z, 2), pl.ds(start, span), :], stage.at[j], sem.at[j])
        for j, z in enumerate((0, n - 2))
    ]
    for copy in copies:
        copy.start()
    for copy in copies:
        copy.wait()
    for m in range(2):
        for comp in range(3):
            for i in range(2):
                below = stage[0, comp, i] if m == 0 else other[comp, i]
                above = stage[1, comp, i] if m == 0 else other[comp, n - 2 + i]
                buf_a[m, comp, i] = jnp.where(parity == 0, above, below)
                buf_b[m, comp, i] = jnp.where(parity == 0, below, above)


def rim_warp_kernel(near, other, buf_a, buf_b):
    parity, _, _ = slab_place()
    n = near.shape[0]
    for m in range(2):
        ref = near if m == 0 else other
        for i in range(2):
            below, above = ref[i], ref[n - 2 + i]
            buf_a[m, i] = jnp.where(parity == 0, above, below)
            buf_b[m, i] = jnp.where(parity == 0, below, above)


def pick(parity, got_a, got_b, high):
    a, b = (got_a, got_b) if high else (got_b, got_a)
    return jnp.where(parity == 0, a, b)


def update(velocity, warped, low, here, high, valid):
    gz = (high - low) * 0.5
    gy = (shift_rows(here, True) - shift_rows(here, False)) * 0.5
    gx = (shift_lanes(here, 1) - shift_lanes(here, -1)) * 0.5
    mismatch = warped + velocity[0] * gz + velocity[1] * gy + velocity[2] * gx - here
    denominator = (gz * gz + gy * gy + gx * gx) + mismatch * mismatch + 1.0
    ratio = mismatch / denominator
    return [jnp.where(valid, v - ratio * g, 0.0) for v, g in zip(velocity, (gz, gy, gx))]


def smooth_plane(v):
    v = (shift_rows(v, False) + 2.0 * v + shift_rows(v, True)) * 0.25
    return (shift_lanes(v, -1) + 2.0 * v + shift_lanes(v, 1)) * 0.25


def first_kernel(
    vel, vel_other, vel_a, vel_b, warp, warp_other, warp_a, warp_b, chip, diag,
    out, out_sum, warps, targets, held, moved, stage, sem,
):
    x, core = chip_and_core()
    parity, has_below, has_above = slab_place()
    n, span = vel_other.shape[1], vel_other.shape[2]
    start = pl.multiple_of(x * (vel.shape[2] - span), 8)
    copy = pltpu.make_async_copy(vel.at[:, :, pl.ds(start, span), :], stage, sem)
    copy.start()
    for i in range(n + 6):
        a, b = chip[i], diag[i]
        targets[0, i] = jnp.where(core == 0, a, b)
        targets[1, i] = jnp.where(core == 0, b, a)
    for m in range(2):
        ref = warp if m == 0 else warp_other
        for i in range(2):
            warps[m, i] = pick(parity, warp_a[m, i], warp_b[m, i], False)
            warps[m, n + 2 + i] = pick(parity, warp_a[m, i], warp_b[m, i], True)
        for i in range(n):
            warps[m, i + 2] = ref[i]
    copy.wait()
    for m in range(2):
        ref = stage if m == 0 else vel_other
        for comp in range(3):
            for i in range(2):
                held[m, comp, i] = pick(parity, vel_a[m, comp, i], vel_b[m, comp, i], False)
                held[m, comp, n + 2 + i] = pick(parity, vel_a[m, comp, i], vel_b[m, comp, i], True)
            for i in range(n):
                held[m, comp, i + 2] = ref[comp, i]
    deep = n + 4

    def step(j, carry):
        m, i = j // deep, j % deep
        valid = (has_below | (i >= 2)) & (has_above | (i < n + 2))
        v = update(
            [held[m, comp, i] for comp in range(3)], warps[m, i],
            targets[m, i], targets[m, i + 1], targets[m, i + 2], valid,
        )
        for comp in range(3):
            moved[m, comp, i] = v[comp]
        return carry

    lax.fori_loop(0, 2 * deep, step, 0)

    def blur(i, carry):
        valid = (has_below | (i >= 1)) & (has_above | (i < n + 1))
        for comp in range(3):
            total = None
            for m in range(2):
                v = (moved[m, comp, i] + 2.0 * moved[m, comp, i + 1] + moved[m, comp, i + 2]) * 0.25
                v = jnp.where(valid, smooth_plane(v), 0.0)
                out[m, comp, i] = v
                total = v if total is None else total + v
            out_sum[comp, i] = total
        return carry

    lax.fori_loop(0, n + 2, blur, 0)


def second_kernel(vel, beside, warps, targets, out, out_sum, moved):
    x, _ = chip_and_core()
    _, has_below, has_above = slab_place()
    n, half = out.shape[2], out.shape[3]
    deep = n + 2

    def step(j, carry):
        m, i = j // deep, j % deep
        valid = (has_below | (i >= 1)) & (has_above | (i < n + 1))
        v = update(
            [(2.0 * vel[m, comp, i] + beside[comp, i]) * 0.25 for comp in range(3)], warps[m, i + 1],
            targets[m, i + 1], targets[m, i + 2], targets[m, i + 3], valid,
        )
        for comp in range(3):
            moved[m, comp, i] = v[comp]
        return carry

    lax.fori_loop(0, 2 * deep, step, 0)

    def blur(i, carry):
        for comp in range(3):
            total = None
            for m in range(2):
                v = (moved[m, comp, i] + 2.0 * moved[m, comp, i + 1] + moved[m, comp, i + 2]) * 0.25
                v = smooth_plane(v)
                v = jnp.where(x == 0, v[:half], v[v.shape[0] - half :])
                out[m, comp, i] = v
                total = v if total is None else total + v
            out_sum[comp, i] = total
        return carry

    lax.fori_loop(0, n, blur, 0)


def send_kernel(vel, beside, out):
    out[...] = (2.0 * vel[1] + beside[...]) * 0.25


def close_kernel(vel, beside, other, out, stage, sem):
    x, _ = chip_and_core()
    half = stage.shape[2]
    there = pltpu.make_async_copy(
        other, out.at[:, :, pl.ds(pl.multiple_of((1 - x) * half, 8), half), :], sem.at[0]
    )
    there.start()
    stage[...] = (2.0 * vel[0] + beside[...]) * 0.25
    here = pltpu.make_async_copy(
        stage, out.at[:, :, pl.ds(pl.multiple_of(x * half, 8), half), :], sem.at[1]
    )
    here.start()
    here.wait()
    there.wait()


def swaps(count, first):
    pairs = []
    for i in range(first, count - 1, 2):
        pairs += [(i, i + 1), (i + 1, i)]
    return pairs


def swap_slabs(buf_a, buf_b):
    count = lax.axis_size("slab")
    return (
        lax.ppermute(buf_a, "slab", swaps(count, 0)),
        lax.ppermute(buf_b, "slab", swaps(count, 1)),
    )


def swap_phases(values, mask):
    return lax.ppermute(values, "phase", [(i, i ^ mask) for i in range(lax.axis_size("phase"))])


def ring_of_four(fine_images, offsets, velocity_init):
    fine, offs, vel = fine_images[0], offsets[0], velocity_init[0]
    deep, tall, wide = fine.shape
    n, rows, cols = offs.shape[1:]
    half = rows // 2
    span = half + RIM
    lanes = 128
    dma = pltpu.SemaphoreType.DMA

    (vel_far,) = launch(cut_kernel, [shape(3, n, span, cols)], [vel], [dma], anys=(0,))
    vel_other = swap_phases(vel_far, 2)

    full = lambda *dims: pl.BlockSpec(dims, lambda k: (0,) * len(dims))
    part, edge, buf_a, buf_b = launch(
        halve_kernel,
        [shape(n, rows, cols), shape(2, rows, cols), shape(4, rows, cols), shape(4, rows, cols)],
        [fine],
        [
            pltpu.VMEM((wide, cols), BF16),
            pltpu.VMEM((cols // lanes, 2 * tall, lanes), F32),
            pltpu.VMEM((rows, cols), F32),
        ],
        grid=(n,),
        in_specs=[pl.BlockSpec((2, tall, wide), lambda k: (k, 0, 0))],
        out_specs=[full(n, rows, cols), full(2, rows, cols), full(4, rows, cols), full(4, rows, cols)],
    )
    got_a, got_b = swap_slabs(buf_a, buf_b)
    ext, near, far = launch(
        join_kernel,
        [shape(n + 6, rows, cols), shape(n + 6, span, cols), shape(n + 6, span, cols)],
        [part, edge, got_a, got_b],
    )
    chip = swap_phases(near, 1)
    diag = swap_phases(far, 3)

    warp, warp_far = launch(
        warp_kernel,
        [shape(n, span, cols), shape(n, span, cols)],
        [ext, offs],
        [
            pltpu.VMEM((5, cols // lanes, n + 4, rows + 16, lanes), F32),
            pltpu.VMEM((n, rows, cols), F32),
        ],
    )
    warp_other = swap_phases(warp_far, 2)

    buf_a, buf_b = launch(
        rim_velocity_kernel,
        [shape(2, 3, 2, span, cols)] * 2,
        [vel, vel_other],
        [pltpu.VMEM((2, 3, 2, span, cols), F32), dma((2,))],
        anys=(0,),
    )
    vel_a, vel_b = swap_slabs(buf_a, buf_b)
    buf_a, buf_b = launch(rim_warp_kernel, [shape(2, 2, span, cols)] * 2, [warp, warp_other])
    warp_a, warp_b = swap_slabs(buf_a, buf_b)

    state, own_sum, warps, targets = launch(
        first_kernel,
        [
            shape(2, 3, n + 2, span, cols),
            shape(3, n + 2, span, cols),
            shape(2, n + 4, span, cols),
            shape(2, n + 6, span, cols),
        ],
        [vel, vel_other, vel_a, vel_b, warp, warp_other, warp_a, warp_b, chip, diag],
        [
            pltpu.VMEM((2, 3, n + 4, span, cols), F32),
            pltpu.VMEM((2, 3, n + 4, span, cols), F32),
            pltpu.VMEM((3, n, span, cols), F32),
            dma,
        ],
        anys=(0,),
    )
    beside = swap_phases(own_sum, 1)
    state, own_sum = launch(
        second_kernel,
        [shape(2, 3, n, half, cols), shape(3, n, half, cols)],
        [state, beside, warps, targets],
        [pltpu.VMEM((2, 3, n + 2, span, cols), F32)],
    )
    beside = swap_phases(own_sum, 1)
    (away,) = launch(send_kernel, [shape(3, n, half, cols)], [state, beside])
    home = swap_phases(away, 2)
    (velocity,) = launch(
        close_kernel,
        [shape(3, n, rows, cols)],
        [state, beside, home],
        [pltpu.VMEM((3, n, half, cols), F32), dma((2,))],
        out_specs=[pl.BlockSpec(memory_space=pl.ANY)],
    )
    return velocity[None]


highest = lax.Precision.HIGHEST


def extended(cells, sides, width):
    for axis, dim in sides:
        count = lax.axis_size(axis)
        ends = count - 1
        head = lax.slice_in_dim(cells, 0, width, axis=dim)
        tail = lax.slice_in_dim(cells, cells.shape[dim] - width, cells.shape[dim], axis=dim)
        cells = jnp.concatenate(
            [
                lax.ppermute(tail, axis, [(i, (i + 1) % count) for i in range(ends)]),
                cells,
                lax.ppermute(head, axis, [((i + 1) % count, i) for i in range(ends)]),
            ],
            axis=dim,
        )
    return cells


def passed_along(block, axis, distance):
    devices = range(lax.axis_size(axis))
    route = [((i - distance) % len(devices), i) for i in devices]
    return lax.ppermute(block, axis, route)


def pad_axis(values, dimension, width):
    widths = [(0, 0)] * values.ndim
    widths[dimension] = (width, width)
    return jnp.pad(values, widths)


def halve_matrix(length):
    fine_index = lax.broadcasted_iota(jnp.int32, (length, length // 2), 0)
    coarse_index = lax.broadcasted_iota(jnp.int32, (length, length // 2), 1)
    outer = (fine_index == 2 * coarse_index - 1) | (fine_index == 2 * coarse_index + 2)
    inner = (fine_index == 2 * coarse_index) | (fine_index == 2 * coarse_index + 1)
    return jnp.where(inner, 0.375, jnp.where(outer, 0.125, 0.0)).astype(jnp.float32)


def smooth_matrix(length):
    source = lax.broadcasted_iota(jnp.int32, (length, length), 0)
    result = lax.broadcasted_iota(jnp.int32, (length, length), 1)
    return jnp.where(
        source == result, 0.5, jnp.where(jnp.abs(source - result) == 1, 0.25, 0.0)
    ).astype(jnp.float32)


def gradient_matrix(length):
    source = lax.broadcasted_iota(jnp.int32, (length, length), 0)
    result = lax.broadcasted_iota(jnp.int32, (length, length), 1)
    return jnp.where(source == result + 1, 0.5, jnp.where(source == result - 1, -0.5, 0.0)).astype(
        jnp.float32
    )


def along_last(values, matrix):
    return jnp.einsum("...j,jk->...k", values, matrix, precision=highest)


def along_rows(values, matrix):
    return jnp.einsum("...jx,jk->...kx", values, matrix, precision=highest)


def halve_depth(values):
    count, depth = (values.shape[0], values.shape[1])
    pairs = values.reshape((count, depth // 2, 2) + values.shape[2:])
    even = pairs[:, :, 0]
    odd = pairs[:, :, 1]
    return (even[:, :-1] + 3.0 * odd[:, :-1] + 3.0 * even[:, 1:] + odd[:, 1:]) * 0.125


def depth_gradient(values):
    length = values.shape[1] - 2
    return (values[:, 2 : 2 + length] - values[:, 0:length]) * 0.5


def depth_smooth(values):
    length = values.shape[2] - 2
    return (
        values[:, :, 0:length] + 2.0 * values[:, :, 1 : 1 + length] + values[:, :, 2 : 2 + length]
    ) * 0.25


def axis_weights(offsets):
    return [
        jnp.where(
            2 * displace == offsets, 1.0, jnp.where(jnp.abs(2 * displace - offsets) == 1, 0.5, 0.0)
        ).astype(jnp.float32)
        for displace in range(-2, 3)
    ]


def warp_moving(moving_rows, offsets):
    layers, height, breadth = (offsets.shape[2], offsets.shape[3], offsets.shape[4])
    weights_z = axis_weights(offsets[:, 0])
    weights_y = axis_weights(offsets[:, 1])
    weights_x = axis_weights(offsets[:, 2])
    shape = offsets[:, 0].shape
    rows_padded = pad_axis(moving_rows, 2, 2)
    wide = pad_axis(rows_padded, 3, 2)
    shifted = [wide[..., index_x : index_x + breadth] for index_x in range(5)]
    warped = jnp.zeros(shape, jnp.float32)
    for index_z in range(5):
        plane_sum = jnp.zeros(shape, jnp.float32)
        for index_y in range(5):
            line_sum = jnp.zeros(shape, jnp.float32)
            for index_x in range(5):
                window = shifted[index_x][:, index_z : index_z + layers, index_y : index_y + height]
                line_sum = line_sum + weights_x[index_x] * window
            plane_sum = plane_sum + weights_y[index_y] * line_sum
        warped = warped + weights_z[index_z] * plane_sum
    return warped


def shards(fine_images, offsets, velocity_init):
    fine_height, fine_breadth = (fine_images.shape[2], fine_images.shape[3])
    rimmed_fine = extended(fine_images, (("slab", 1),), 1)
    coarse = halve_depth(rimmed_fine)
    coarse = along_rows(coarse, halve_matrix(fine_height))
    coarse = along_last(coarse, halve_matrix(fine_breadth))
    target = passed_along(coarse, "phase", -1)
    height, breadth = (coarse.shape[2], coarse.shape[3])
    moving_rows = extended(coarse, (("slab", 1),), 2)
    target_rows = extended(target, (("slab", 1),), 1)
    grad_z = depth_gradient(target_rows)
    grad_y = along_rows(target, gradient_matrix(height))
    grad_x = along_last(target, gradient_matrix(breadth))
    gradients = jnp.stack([grad_z, grad_y, grad_x], axis=1)
    norm_squared = grad_z * grad_z + grad_y * grad_y + grad_x * grad_x
    warped_base = warp_moving(moving_rows, offsets)
    smooth_rows = smooth_matrix(height)
    smooth_columns = smooth_matrix(breadth)
    velocity = velocity_init
    for iteration in range(ITERS):
        warped = (
            warped_base
            + velocity[:, 0] * grad_z
            + velocity[:, 1] * grad_y
            + velocity[:, 2] * grad_x
        )
        mismatch = warped - target
        denominator = norm_squared + mismatch * mismatch + 1.0
        velocity = velocity - (mismatch / denominator)[:, None] * gradients
        rimmed = extended(velocity, (("slab", 2),), 1)
        velocity = depth_smooth(rimmed)
        velocity = along_rows(velocity, smooth_rows)
        velocity = along_last(velocity, smooth_columns)
        earlier = passed_along(velocity, "phase", 1)
        later = passed_along(velocity, "phase", -1)
        velocity = (earlier + 2.0 * velocity + later) * 0.25
    return velocity


def solution(mesh):
    placed = (
        P(("case", "phase"), "slab", None, None),
        P(("case", "phase"), None, "slab", None, None),
        P(("case", "phase"), None, "slab", None, None),
    )
    return jax.shard_map(
        ring_of_four if mesh.shape["phase"] == 4 else shards,
        mesh=mesh,
        in_specs=placed,
        out_specs=P(("case", "phase"), None, "slab", None, None),
        check_vma=False,
    )
```

```python
import jax
import jax.numpy as jnp
from jax import lax
from jax.experimental import pallas as pl
from jax.experimental.pallas import tpu as pltpu
from jax.sharding import PartitionSpec as P


ITERS = 2
RIM = 8
F32 = jnp.float32
BF16 = jnp.bfloat16


def launch(body, outs, ins, scratch=(), hbm=(), hbm_out=(), micros=1.0, limit=16, alias={}):
    spaces = [pltpu.HBM if i in hbm else pltpu.VMEM for i in range(len(ins))]
    targets = [pl.ANY if i in hbm_out else pltpu.VMEM for i in range(len(outs))]
    return pl.pallas_call(
        body,
        out_shape=outs,
        in_specs=[pl.BlockSpec(memory_space=space) for space in spaces],
        out_specs=[pl.BlockSpec(memory_space=space) for space in targets],
        scratch_shapes=scratch,
        input_output_aliases=alias,
        compiler_params=pltpu.CompilerParams(vmem_limit_bytes=limit * 2**20),
        cost_estimate=pl.CostEstimate(
            flops=0, bytes_accessed=int(micros * 3.3e6), transcendentals=0
        ),
    )(*[pltpu.with_memory_space_constraint(v, pltpu.HBM) if i in hbm and i not in alias else v for i, v in enumerate(ins)])


def shape(*dims):
    return jax.ShapeDtypeStruct(dims, F32)


def chip_and_core():
    phase = lax.axis_index("phase")
    return phase // 2, phase % 2


def slab_place():
    slab = lax.axis_index("slab")
    last = lax.axis_size("slab") - 1
    return slab % 2, slab > 0, slab < last


def shift_rows(a, up):
    zero = jnp.zeros((1, a.shape[1]), a.dtype)
    return jnp.concatenate([a[1:], zero], 0) if up else jnp.concatenate([zero, a[:-1]], 0)


def shift_lanes(a, step):
    width = a.shape[1]
    lane = lax.broadcasted_iota(jnp.int32, a.shape, 1)
    moved = pltpu.roll(a, (-step) % width, 1)
    keep = lane < width - step if step > 0 else lane >= -step
    return jnp.where(keep, moved, 0.0)


def halve_kernel(fine, part, edge, buf_a, buf_b, held, mat, rows, prev, sems):
    count, tall, wide = fine.shape
    n, half = count // 2, tall // 2
    cut = rows.shape[2]

    def fetch(k):
        pair = pl.ds(2 * k, 2)
        return pltpu.make_async_copy(fine.at[pair], held.at[pair], sems.at[k])

    for k in range(n):
        fetch(k).start()
    i = lax.broadcasted_iota(jnp.int32, mat.shape, 0)
    j = lax.broadcasted_iota(jnp.int32, mat.shape, 1)
    d = i - 2 * j
    inner = (d == 0) | (d == 1)
    outer = (d == -1) | (d == 2)
    mat[...] = jnp.where(inner, 0.375, jnp.where(outer, 0.125, 0.0)).astype(BF16)

    def pair(k, carry):
        fetch(k).wait()
        f = held[pl.ds(2 * k, 2)].reshape(2 * tall, wide)
        hi = f.astype(BF16)
        lo = (f - hi.astype(F32)).astype(BF16)
        w = mat[...]
        got = jnp.dot(hi, w, preferred_element_type=F32)
        got += jnp.dot(lo, w, preferred_element_type=F32)
        for c in range(rows.shape[0]):
            rows[c] = got[:, c * cut : (c + 1) * cut]
        layers = []
        for z in range(2):
            cols = []
            for c in range(rows.shape[0]):
                even = rows[c, pl.ds(z * tall, half, 2), :]
                odd = rows[c, pl.ds(z * tall + 1, half, 2), :]
                cols.append(
                    (shift_rows(odd, False) + shift_rows(even, True) + 3.0 * (even + odd))
                    * (1.0 / 64.0)
                )
            layers.append(jnp.concatenate(cols, 1))
        even, odd = layers
        mid = 3.0 * (even + odd)

        @pl.when(k == 0)
        def _():
            edge[0] = even
            part[0] = mid

        @pl.when(k > 0)
        def _():
            part[k] = mid + prev[...]
            part[k - 1] += even

        prev[...] = odd
        return carry

    lax.fori_loop(0, n, pair, 0)
    edge[1] = prev[...]
    parity, _, _ = slab_place()
    for i in range(4):
        above = edge[1] if i == 3 else part[n - 3 + i]
        below = edge[0] if i == 0 else part[i - 1]
        buf_a[i] = jnp.where(parity == 0, above, below)
        buf_b[i] = jnp.where(parity == 0, below, above)


def pack(dst, layer, count, chip, half):
    low = lax.broadcasted_iota(jnp.int32, (8, dst.shape[1]), 0) < 4
    mine = low == (chip == 0)
    main = pl.multiple_of(8 * chip, 8)
    rim = pl.multiple_of(half * (1 - chip), 8)
    for i in range(count):
        dst[pl.ds(i * half, half), :] = layer(i, main, half)
    for i in range(0, count, 2):
        a, b = layer(i, rim, 8), layer(i + 1, rim, 8)
        dst[pl.ds(count * half + 4 * i, 8), :] = jnp.where(mine, a, pltpu.roll(b, 4, 0))


def unpack(src, store, count, chip, half):
    main = pl.multiple_of(8 * chip, 8)
    rim = pl.multiple_of(half * (1 - chip), 8)
    for i in range(count):
        store(i, main, half, src[pl.ds(i * half, half), :])
    for i in range(0, count, 2):
        v = src[pl.ds(count * half + 4 * i, 8), :]
        store(i, rim, 8, v)
        store(i + 1, rim, 8, pltpu.roll(v, 4, 0))


def join_kernel(part, edge, got_a, got_b, ext, near, far):
    n = part.shape[0]
    parity, has_below, has_above = slab_place()
    x, _ = chip_and_core()
    for i in range(3):
        low = jnp.where(parity == 0, got_b[i], got_a[i])
        high = jnp.where(parity == 0, got_a[i + 1], got_b[i + 1])
        if i == 2:
            low = jnp.where(has_below, low + edge[0], 0.0)
        if i == 0:
            high = jnp.where(has_above, high + edge[1], 0.0)
        ext[i] = low
        ext[n + 3 + i] = high
    for i in range(n):
        v = part[i]
        if i == 0:
            v = v + jnp.where(parity == 0, got_b[3], got_a[3])
        if i == n - 1:
            v = v + jnp.where(parity == 0, got_a[0], got_b[0])
        ext[i + 3] = v
    span = near.shape[1]
    step = ext.shape[1] - span
    near[...] = ext[:, pl.ds(pl.multiple_of(x * step, 8), span), :]
    there = (1 - x) * step

    def layer(i, start, size):
        return ext[i + 3, pl.ds(pl.multiple_of(there + start, 8), size), :]

    pack(far, layer, n, 1 - x, ext.shape[1] // 2)


def warp_kernel(ext, offs, near, far, wide, full):
    n, tall = offs.shape[1], ext.shape[1]
    depth = n + 4
    columns, lanes = wide.shape[1], wide.shape[4]
    blank = jnp.zeros((8, lanes), F32)

    def fill(z, carry):
        v = ext[z + 1]
        for s in range(5):
            moved = v if s == 2 else shift_lanes(v, s - 2)
            for c in range(columns):
                wide[s, c, z, pl.ds(0, 8), :] = blank
                wide[s, c, z, pl.ds(8, tall), :] = moved[:, c * lanes : (c + 1) * lanes]
                wide[s, c, z, pl.ds(8 + tall, 8), :] = blank
        return carry

    lax.fori_loop(0, depth, fill, 0)

    def weights(comp, z, y, c):
        h = offs[comp, z, pl.ds(y, 8), pl.ds(c * lanes, lanes)].astype(F32) * 0.5
        return [jnp.maximum(1.0 - jnp.abs(h - (s - 2.0)), 0.0) for s in range(5)]

    def tile(i, carry):
        z = i // (tall // 8)
        y = pl.multiple_of((i % (tall // 8)) * 8, 8)
        for c in range(columns):
            wz, wy, wx = (weights(m, z, y, c) for m in range(3))
            total = None
            for a in range(5):
                plane = None
                for b in range(5):
                    line = None
                    for s in range(5):
                        term = wx[s] * wide[s, c, z + a, pl.ds(y + 6 + b, 8), :]
                        line = term if line is None else line + term
                    line = wy[b] * line
                    plane = line if plane is None else plane + line
                plane = wz[a] * plane
                total = plane if total is None else total + plane
            full[z, pl.ds(y, 8), pl.ds(c * lanes, lanes)] = total
        return carry

    lax.fori_loop(0, n * (tall // 8), tile, 0)
    x, _ = chip_and_core()
    span = near.shape[1]
    step = tall - span
    near[...] = full[:, pl.ds(pl.multiple_of(x * step, 8), span), :]
    there = (1 - x) * step

    def layer(i, start, size):
        return full[i, pl.ds(pl.multiple_of(there + start, 8), size), :]

    pack(far, layer, n, 1 - x, tall // 2)


def cut_kernel(vel, far, held, sem):
    x, _ = chip_and_core()
    n, tall = vel.shape[1:3]
    span = held.shape[2]
    there = pl.multiple_of((1 - x) * (tall - span), 8)
    copy = pltpu.make_async_copy(vel.at[:, :, pl.ds(there, span), :], held, sem)
    copy.start()
    copy.wait()

    def layer(i, start, size):
        return held[i // n, i % n, pl.ds(start, size), :]

    pack(far, layer, 3 * n, 1 - x, tall // 2)


def rim_own_kernel(vel, buf_a, buf_b, stage, sem):
    x, _ = chip_and_core()
    parity, _, _ = slab_place()
    n = vel.shape[1]
    span = stage.shape[3]
    start = pl.multiple_of(x * (vel.shape[2] - span), 8)
    copies = [
        pltpu.make_async_copy(vel.at[:, pl.ds(z, 2), pl.ds(start, span), :], stage.at[j], sem.at[j])
        for j, z in enumerate((0, n - 2))
    ]
    for copy in copies:
        copy.start()
    for copy in copies:
        copy.wait()
    below, above = stage[0], stage[1]
    buf_a[...] = jnp.where(parity == 0, above, below)
    buf_b[...] = jnp.where(parity == 0, below, above)


def rim_other_kernel(vel_far, diag_far, buf_a, buf_b, vel_other, diag):
    x, _ = chip_and_core()
    parity, _, _ = slab_place()
    n, span = vel_other.shape[1:3]
    half = span - RIM

    def store_vel(i, start, size, v):
        vel_other[i // n, i % n, pl.ds(start, size), :] = v

    def store_diag(i, start, size, v):
        diag[i, pl.ds(start, size), :] = v

    unpack(vel_far, store_vel, 3 * n, x, half)
    unpack(diag_far, store_diag, n, x, half)
    for comp in range(3):
        for i in range(2):
            below, above = vel_other[comp, i], vel_other[comp, n - 2 + i]
            buf_a[2 * comp + i] = jnp.where(parity == 0, above, below)
            buf_b[2 * comp + i] = jnp.where(parity == 0, below, above)
    for i in range(3):
        below, above = diag[i], diag[n - 3 + i]
        buf_a[6 + i] = jnp.where(parity == 0, above, below)
        buf_b[6 + i] = jnp.where(parity == 0, below, above)


def rim_warp_kernel(near, far, buf_a, buf_b, other):
    x, _ = chip_and_core()
    parity, _, _ = slab_place()
    n, span = near.shape[:2]

    def store(i, start, size, v):
        other[i, pl.ds(start, size), :] = v

    unpack(far, store, n, x, span - RIM)
    for m in range(2):
        ref = near if m == 0 else other
        for i in range(2):
            below, above = ref[i], ref[n - 2 + i]
            buf_a[m, i] = jnp.where(parity == 0, above, below)
            buf_b[m, i] = jnp.where(parity == 0, below, above)


def pick(parity, got_a, got_b, high):
    a, b = (got_a, got_b) if high else (got_b, got_a)
    return jnp.where(parity == 0, a, b)


def update(velocity, warped, low, here, high, valid):
    gz = (high - low) * 0.5
    gy = (shift_rows(here, True) - shift_rows(here, False)) * 0.5
    gx = (shift_lanes(here, 1) - shift_lanes(here, -1)) * 0.5
    mismatch = warped + velocity[0] * gz + velocity[1] * gy + velocity[2] * gx - here
    denominator = (gz * gz + gy * gy + gx * gx) + mismatch * mismatch + 1.0
    ratio = mismatch / denominator
    return [jnp.where(valid, v - ratio * g, 0.0) for v, g in zip(velocity, (gz, gy, gx))]


def smooth_plane(v):
    v = (shift_rows(v, False) + 2.0 * v + shift_rows(v, True)) * 0.25
    return (shift_lanes(v, -1) + 2.0 * v + shift_lanes(v, 1)) * 0.25


def first_kernel(
    vel, vel_other, own_a, own_b, rim_a, rim_b, warp, warp_other, warp_a, warp_b, chip, diag,
    out, out_sum, warps, targets, held, moved, stage, sem,
):
    x, core = chip_and_core()
    parity, has_below, has_above = slab_place()
    n, span = vel_other.shape[1], vel_other.shape[2]
    start = pl.multiple_of(x * (vel.shape[2] - span), 8)
    copy = pltpu.make_async_copy(vel.at[:, :, pl.ds(start, span), :], stage, sem)
    copy.start()
    for i in range(n + 6):
        a = chip[i]
        if i < 3:
            b = pick(parity, rim_a[6 + i], rim_b[6 + i], False)
        elif i < n + 3:
            b = diag[i - 3]
        else:
            b = pick(parity, rim_a[3 + i - n], rim_b[3 + i - n], True)
        targets[0, i] = jnp.where(core == 0, a, b)
        targets[1, i] = jnp.where(core == 0, b, a)
    for m in range(2):
        ref = warp if m == 0 else warp_other
        for i in range(2):
            warps[m, i] = pick(parity, warp_a[m, i], warp_b[m, i], False)
            warps[m, n + 2 + i] = pick(parity, warp_a[m, i], warp_b[m, i], True)
        for i in range(n):
            warps[m, i + 2] = ref[i]
    copy.wait()
    for m in range(2):
        ref = stage if m == 0 else vel_other
        for comp in range(3):
            for i in range(2):
                a, b = (own_a[comp, i], own_b[comp, i]) if m == 0 else (rim_a[2 * comp + i], rim_b[2 * comp + i])
                held[m, comp, i] = pick(parity, a, b, False)
                held[m, comp, n + 2 + i] = pick(parity, a, b, True)
            for i in range(n):
                held[m, comp, i + 2] = ref[comp, i]
    deep = n + 4

    def step(j, carry):
        m, i = j // deep, j % deep
        valid = (has_below | (i >= 2)) & (has_above | (i < n + 2))
        v = update(
            [held[m, comp, i] for comp in range(3)], warps[m, i],
            targets[m, i], targets[m, i + 1], targets[m, i + 2], valid,
        )
        for comp in range(3):
            moved[m, comp, i] = v[comp]
        return carry

    lax.fori_loop(0, 2 * deep, step, 0)

    def blur(i, carry):
        valid = (has_below | (i >= 1)) & (has_above | (i < n + 1))
        for comp in range(3):
            total = None
            for m in range(2):
                v = (moved[m, comp, i] + 2.0 * moved[m, comp, i + 1] + moved[m, comp, i + 2]) * 0.25
                v = jnp.where(valid, smooth_plane(v), 0.0)
                out[m, comp, i] = v
                total = v if total is None else total + v
            out_sum[comp, i] = total
        return carry

    lax.fori_loop(0, n + 2, blur, 0)


def second_kernel(vel, beside, warps, targets, out, out_sum, moved):
    x, _ = chip_and_core()
    _, has_below, has_above = slab_place()
    n, half = out.shape[2], out.shape[3]
    deep = n + 2

    def step(j, carry):
        m, i = j // deep, j % deep
        valid = (has_below | (i >= 1)) & (has_above | (i < n + 1))
        v = update(
            [(2.0 * vel[m, comp, i] + beside[comp, i]) * 0.25 for comp in range(3)], warps[m, i + 1],
            targets[m, i + 1], targets[m, i + 2], targets[m, i + 3], valid,
        )
        for comp in range(3):
            moved[m, comp, i] = v[comp]
        return carry

    lax.fori_loop(0, 2 * deep, step, 0)

    def blur(i, carry):
        for comp in range(3):
            total = None
            for m in range(2):
                v = (moved[m, comp, i] + 2.0 * moved[m, comp, i + 1] + moved[m, comp, i + 2]) * 0.25
                v = smooth_plane(v)
                v = jnp.where(x == 0, v[:half], v[v.shape[0] - half :])
                out[m, comp, i] = v
                total = v if total is None else total + v
            out_sum[comp, i] = total
        return carry

    lax.fori_loop(0, n, blur, 0)


def send_kernel(vel, beside, out):
    out[...] = (2.0 * vel[1] + beside[...]) * 0.25


def close_own_kernel(vel, beside, out, stage, sem):
    x, _ = chip_and_core()
    half = stage.shape[2]
    stage[...] = (2.0 * vel[0] + beside[...]) * 0.25
    here = pltpu.make_async_copy(
        stage, out.at[:, :, pl.ds(pl.multiple_of(x * half, 8), half), :], sem
    )
    here.start()
    here.wait()


def close_far_kernel(done, home, out, sem):
    del done
    x, _ = chip_and_core()
    half = home.shape[2]
    there = pltpu.make_async_copy(
        home, out.at[:, :, pl.ds(pl.multiple_of((1 - x) * half, 8), half), :], sem
    )
    there.start()
    there.wait()


def swaps(count, first):
    pairs = []
    for i in range(first, count - 1, 2):
        pairs += [(i, i + 1), (i + 1, i)]
    return pairs


def swap_slabs(buf_a, buf_b):
    count = lax.axis_size("slab")
    got_a = lax.ppermute(buf_a, "slab", swaps(count, 0))
    got_b = lax.ppermute(buf_b, "slab", swaps(count, 1))
    return got_a, got_b


def swap_phases(values, mask):
    return lax.ppermute(values, "phase", [(i, i ^ mask) for i in range(lax.axis_size("phase"))])


def ring_of_four(fine_images, offsets, velocity_init):
    return four_phases(fine_images, offsets, velocity_init)


def four_phases(fine_images, offsets, velocity_init):
    fine, offs, vel = fine_images[0], offsets[0], velocity_init[0]
    deep, tall, wide = fine.shape
    n, rows, cols = offs.shape[1:]
    half = rows // 2
    span = half + RIM
    lanes = 128
    dma = pltpu.SemaphoreType.DMA

    (vel_cut,) = launch(
        cut_kernel,
        [shape(3 * n * (half + 4), cols)],
        [vel],
        [pltpu.VMEM((3, n, span, cols), F32), dma],
        hbm=(0,),
        micros=1.0,
    )
    vel_far = swap_phases(vel_cut, 2)

    part, edge, buf_a, buf_b = launch(
        halve_kernel,
        [shape(n, rows, cols), shape(2, rows, cols), shape(4, rows, cols), shape(4, rows, cols)],
        [fine],
        [
            pltpu.VMEM((deep, tall, wide), F32),
            pltpu.VMEM((wide, cols), BF16),
            pltpu.VMEM((cols // lanes, 2 * tall, lanes), F32),
            pltpu.VMEM((rows, cols), F32),
            dma((n,)),
        ],
        hbm=(0,),
        micros=4.0,
    )
    got_a, got_b = swap_slabs(buf_a, buf_b)
    buf_a, buf_b = launch(
        rim_own_kernel,
        [shape(3, 2, span, cols)] * 2,
        [vel],
        [pltpu.VMEM((2, 3, 2, span, cols), F32), dma((2,))],
        hbm=(0,),
    )
    own_a, own_b = swap_slabs(buf_a, buf_b)
    ext, near, far = launch(
        join_kernel,
        [shape(n + 6, rows, cols), shape(n + 6, span, cols), shape(n * (half + 4), cols)],
        [part, edge, got_a, got_b],
    )
    chip = swap_phases(near, 1)
    diag_far = swap_phases(far, 3)

    warp, warp_cut = launch(
        warp_kernel,
        [shape(n, span, cols), shape(n * (half + 4), cols)],
        [ext, offs],
        [
            pltpu.VMEM((5, cols // lanes, n + 4, rows + 16, lanes), F32),
            pltpu.VMEM((n, rows, cols), F32),
        ],
        micros=8.5,
    )
    warp_far = swap_phases(warp_cut, 2)

    buf_a, buf_b, vel_other, diag = launch(
        rim_other_kernel,
        [shape(9, span, cols)] * 2 + [shape(3, n, span, cols), shape(n, span, cols)],
        [vel_far, diag_far],
    )
    rim_a, rim_b = swap_slabs(buf_a, buf_b)
    buf_a, buf_b, warp_other = launch(
        rim_warp_kernel,
        [shape(2, 2, span, cols)] * 2 + [shape(n, span, cols)],
        [warp, warp_far],
    )
    warp_a, warp_b = swap_slabs(buf_a, buf_b)

    state, own_sum, warps, targets = launch(
        first_kernel,
        [
            shape(2, 3, n + 2, span, cols),
            shape(3, n + 2, span, cols),
            shape(2, n + 4, span, cols),
            shape(2, n + 6, span, cols),
        ],
        [vel, vel_other, own_a, own_b, rim_a, rim_b, warp, warp_other, warp_a, warp_b, chip, diag],
        [
            pltpu.VMEM((2, 3, n + 4, span, cols), F32),
            pltpu.VMEM((2, 3, n + 4, span, cols), F32),
            pltpu.VMEM((3, n, span, cols), F32),
            dma,
        ],
        hbm=(0,),
        micros=5.0,
    )
    beside = swap_phases(own_sum, 1)
    state, own_sum = launch(
        second_kernel,
        [shape(2, 3, n, half, cols), shape(3, n, half, cols)],
        [state, beside, warps, targets],
        [pltpu.VMEM((2, 3, n + 2, span, cols), F32)],
        micros=4.0,
    )
    beside = swap_phases(own_sum, 1)
    (away,) = launch(send_kernel, [shape(3, n, half, cols)], [state, beside])
    home = swap_phases(away, 2)
    (velocity,) = launch(
        close_own_kernel,
        [shape(3, n, rows, cols)],
        [state, beside],
        [pltpu.VMEM((3, n, half, cols), F32), dma],
        hbm_out=(0,),
    )
    (velocity,) = launch(
        close_far_kernel,
        [shape(3, n, rows, cols)],
        [velocity, home],
        [dma],
        hbm=(0,),
        hbm_out=(0,),
        alias={0: 0},
    )
    return velocity[None]


highest = lax.Precision.HIGHEST


def extended(cells, sides, width):
    for axis, dim in sides:
        count = lax.axis_size(axis)
        ends = count - 1
        head = lax.slice_in_dim(cells, 0, width, axis=dim)
        tail = lax.slice_in_dim(cells, cells.shape[dim] - width, cells.shape[dim], axis=dim)
        cells = jnp.concatenate(
            [
                lax.ppermute(tail, axis, [(i, (i + 1) % count) for i in range(ends)]),
                cells,
                lax.ppermute(head, axis, [((i + 1) % count, i) for i in range(ends)]),
            ],
            axis=dim,
        )
    return cells


def passed_along(block, axis, distance):
    devices = range(lax.axis_size(axis))
    route = [((i - distance) % len(devices), i) for i in devices]
    return lax.ppermute(block, axis, route)


def pad_axis(values, dimension, width):
    widths = [(0, 0)] * values.ndim
    widths[dimension] = (width, width)
    return jnp.pad(values, widths)


def halve_matrix(length):
    fine_index = lax.broadcasted_iota(jnp.int32, (length, length // 2), 0)
    coarse_index = lax.broadcasted_iota(jnp.int32, (length, length // 2), 1)
    outer = (fine_index == 2 * coarse_index - 1) | (fine_index == 2 * coarse_index + 2)
    inner = (fine_index == 2 * coarse_index) | (fine_index == 2 * coarse_index + 1)
    return jnp.where(inner, 0.375, jnp.where(outer, 0.125, 0.0)).astype(jnp.float32)


def smooth_matrix(length):
    source = lax.broadcasted_iota(jnp.int32, (length, length), 0)
    result = lax.broadcasted_iota(jnp.int32, (length, length), 1)
    return jnp.where(
        source == result, 0.5, jnp.where(jnp.abs(source - result) == 1, 0.25, 0.0)
    ).astype(jnp.float32)


def gradient_matrix(length):
    source = lax.broadcasted_iota(jnp.int32, (length, length), 0)
    result = lax.broadcasted_iota(jnp.int32, (length, length), 1)
    return jnp.where(source == result + 1, 0.5, jnp.where(source == result - 1, -0.5, 0.0)).astype(
        jnp.float32
    )


def along_last(values, matrix):
    return jnp.einsum("...j,jk->...k", values, matrix, precision=highest)


def along_rows(values, matrix):
    return jnp.einsum("...jx,jk->...kx", values, matrix, precision=highest)


def halve_depth(values):
    count, depth = (values.shape[0], values.shape[1])
    pairs = values.reshape((count, depth // 2, 2) + values.shape[2:])
    even = pairs[:, :, 0]
    odd = pairs[:, :, 1]
    return (even[:, :-1] + 3.0 * odd[:, :-1] + 3.0 * even[:, 1:] + odd[:, 1:]) * 0.125


def depth_gradient(values):
    length = values.shape[1] - 2
    return (values[:, 2 : 2 + length] - values[:, 0:length]) * 0.5


def depth_smooth(values):
    length = values.shape[2] - 2
    return (
        values[:, :, 0:length] + 2.0 * values[:, :, 1 : 1 + length] + values[:, :, 2 : 2 + length]
    ) * 0.25


def axis_weights(offsets):
    return [
        jnp.where(
            2 * displace == offsets, 1.0, jnp.where(jnp.abs(2 * displace - offsets) == 1, 0.5, 0.0)
        ).astype(jnp.float32)
        for displace in range(-2, 3)
    ]


def warp_moving(moving_rows, offsets):
    layers, height, breadth = (offsets.shape[2], offsets.shape[3], offsets.shape[4])
    weights_z = axis_weights(offsets[:, 0])
    weights_y = axis_weights(offsets[:, 1])
    weights_x = axis_weights(offsets[:, 2])
    shape = offsets[:, 0].shape
    rows_padded = pad_axis(moving_rows, 2, 2)
    wide = pad_axis(rows_padded, 3, 2)
    shifted = [wide[..., index_x : index_x + breadth] for index_x in range(5)]
    warped = jnp.zeros(shape, jnp.float32)
    for index_z in range(5):
        plane_sum = jnp.zeros(shape, jnp.float32)
        for index_y in range(5):
            line_sum = jnp.zeros(shape, jnp.float32)
            for index_x in range(5):
                window = shifted[index_x][:, index_z : index_z + layers, index_y : index_y + height]
                line_sum = line_sum + weights_x[index_x] * window
            plane_sum = plane_sum + weights_y[index_y] * line_sum
        warped = warped + weights_z[index_z] * plane_sum
    return warped


def shards(fine_images, offsets, velocity_init):
    fine_height, fine_breadth = (fine_images.shape[2], fine_images.shape[3])
    rimmed_fine = extended(fine_images, (("slab", 1),), 1)
    coarse = halve_depth(rimmed_fine)
    coarse = along_rows(coarse, halve_matrix(fine_height))
    coarse = along_last(coarse, halve_matrix(fine_breadth))
    target = passed_along(coarse, "phase", -1)
    height, breadth = (coarse.shape[2], coarse.shape[3])
    moving_rows = extended(coarse, (("slab", 1),), 2)
    target_rows = extended(target, (("slab", 1),), 1)
    grad_z = depth_gradient(target_rows)
    grad_y = along_rows(target, gradient_matrix(height))
    grad_x = along_last(target, gradient_matrix(breadth))
    gradients = jnp.stack([grad_z, grad_y, grad_x], axis=1)
    norm_squared = grad_z * grad_z + grad_y * grad_y + grad_x * grad_x
    warped_base = warp_moving(moving_rows, offsets)
    smooth_rows = smooth_matrix(height)
    smooth_columns = smooth_matrix(breadth)
    velocity = velocity_init
    for _ in range(ITERS):
        warped = (
            warped_base
            + velocity[:, 0] * grad_z
            + velocity[:, 1] * grad_y
            + velocity[:, 2] * grad_x
        )
        mismatch = warped - target
        denominator = norm_squared + mismatch * mismatch + 1.0
        velocity = velocity - (mismatch / denominator)[:, None] * gradients
        rimmed = extended(velocity, (("slab", 2),), 1)
        velocity = depth_smooth(rimmed)
        velocity = along_rows(velocity, smooth_rows)
        velocity = along_last(velocity, smooth_columns)
        earlier = passed_along(velocity, "phase", 1)
        later = passed_along(velocity, "phase", -1)
        velocity = (earlier + 2.0 * velocity + later) * 0.25
    return velocity


def solution(mesh):
    placed = (
        P(("case", "phase"), "slab", None, None),
        P(("case", "phase"), None, "slab", None, None),
        P(("case", "phase"), None, "slab", None, None),
    )
    four = mesh.shape["phase"] == 4
    return jax.shard_map(
        ring_of_four if four else shards,
        mesh=mesh,
        in_specs=placed,
        out_specs=P(("case", "phase"), None, "slab", None, None),
        check_vma=False,
    )
```

```python
import jax
import jax.numpy as jnp
from jax import lax
from jax.experimental import pallas as pl
from jax.experimental.pallas import tpu as pltpu
from jax.sharding import PartitionSpec as P


ITERS = 2
RIM = 8
F32 = jnp.float32
BF16 = jnp.bfloat16


def launch(body, outs, ins, scratch=(), hbm=(), hbm_out=(), micros=1.0, limit=16, alias={}):
    spaces = [pltpu.HBM if i in hbm else pltpu.VMEM for i in range(len(ins))]
    targets = [pl.ANY if i in hbm_out else pltpu.VMEM for i in range(len(outs))]
    return pl.pallas_call(
        body,
        out_shape=outs,
        in_specs=[pl.BlockSpec(memory_space=space) for space in spaces],
        out_specs=[pl.BlockSpec(memory_space=space) for space in targets],
        scratch_shapes=scratch,
        input_output_aliases=alias,
        compiler_params=pltpu.CompilerParams(vmem_limit_bytes=limit * 2**20),
        cost_estimate=pl.CostEstimate(
            flops=0, bytes_accessed=int(micros * 3.3e6), transcendentals=0
        ),
    )(*[pltpu.with_memory_space_constraint(v, pltpu.HBM) if i in hbm and i not in alias else v for i, v in enumerate(ins)])


def shape(*dims):
    return jax.ShapeDtypeStruct(dims, F32)


def chip_and_core():
    phase = lax.axis_index("phase")
    return phase // 2, phase % 2


def slab_place():
    slab = lax.axis_index("slab")
    last = lax.axis_size("slab") - 1
    return slab % 2, slab > 0, slab < last


def shift_rows(a, up):
    zero = jnp.zeros((1, a.shape[1]), a.dtype)
    return jnp.concatenate([a[1:], zero], 0) if up else jnp.concatenate([zero, a[:-1]], 0)


def shift_lanes(a, step):
    width = a.shape[1]
    lane = lax.broadcasted_iota(jnp.int32, a.shape, 1)
    moved = pltpu.roll(a, (-step) % width, 1)
    keep = lane < width - step if step > 0 else lane >= -step
    return jnp.where(keep, moved, 0.0)


def halve_kernel(fine, part, edge, buf_a, buf_b, held, mat, rows, prev, sems):
    count, tall, wide = fine.shape
    n, half = count // 2, tall // 2
    cut = rows.shape[2]

    def fetch(k):
        pair = pl.ds(2 * k, 2)
        return pltpu.make_async_copy(fine.at[pair], held.at[pair], sems.at[k])

    for k in range(n):
        fetch(k).start()
    i = lax.broadcasted_iota(jnp.int32, mat.shape, 0)
    j = lax.broadcasted_iota(jnp.int32, mat.shape, 1)
    d = i - 2 * j
    inner = (d == 0) | (d == 1)
    outer = (d == -1) | (d == 2)
    mat[...] = jnp.where(inner, 0.375, jnp.where(outer, 0.125, 0.0)).astype(BF16)

    def pair(k, carry):
        fetch(k).wait()
        f = held[pl.ds(2 * k, 2)].reshape(2 * tall, wide)
        hi = f.astype(BF16)
        lo = (f - hi.astype(F32)).astype(BF16)
        w = mat[...]
        got = jnp.dot(hi, w, preferred_element_type=F32)
        got += jnp.dot(lo, w, preferred_element_type=F32)
        for c in range(rows.shape[0]):
            rows[c] = got[:, c * cut : (c + 1) * cut]
        layers = []
        for z in range(2):
            cols = []
            for c in range(rows.shape[0]):
                even = rows[c, pl.ds(z * tall, half, 2), :]
                odd = rows[c, pl.ds(z * tall + 1, half, 2), :]
                cols.append(
                    (shift_rows(odd, False) + shift_rows(even, True) + 3.0 * (even + odd))
                    * (1.0 / 64.0)
                )
            layers.append(jnp.concatenate(cols, 1))
        even, odd = layers
        mid = 3.0 * (even + odd)

        @pl.when(k == 0)
        def _():
            edge[0] = even
            part[0] = mid

        @pl.when(k > 0)
        def _():
            part[k] = mid + prev[...]
            part[k - 1] += even

        prev[...] = odd
        return carry

    lax.fori_loop(0, n, pair, 0)
    edge[1] = prev[...]
    parity, _, _ = slab_place()
    for i in range(4):
        above = edge[1] if i == 3 else part[n - 3 + i]
        below = edge[0] if i == 0 else part[i - 1]
        buf_a[i] = jnp.where(parity == 0, above, below)
        buf_b[i] = jnp.where(parity == 0, below, above)


def pack(dst, layer, count, chip, half):
    low = lax.broadcasted_iota(jnp.int32, (8, dst.shape[1]), 0) < 4
    mine = low == (chip == 0)
    main = pl.multiple_of(8 * chip, 8)
    rim = pl.multiple_of(half * (1 - chip), 8)
    for i in range(count):
        dst[pl.ds(i * half, half), :] = layer(i, main, half)
    for i in range(0, count, 2):
        a, b = layer(i, rim, 8), layer(i + 1, rim, 8)
        dst[pl.ds(count * half + 4 * i, 8), :] = jnp.where(mine, a, pltpu.roll(b, 4, 0))


def unpack(src, store, count, chip, half):
    main = pl.multiple_of(8 * chip, 8)
    rim = pl.multiple_of(half * (1 - chip), 8)
    for i in range(count):
        store(i, main, half, src[pl.ds(i * half, half), :])
    for i in range(0, count, 2):
        v = src[pl.ds(count * half + 4 * i, 8), :]
        store(i, rim, 8, v)
        store(i + 1, rim, 8, pltpu.roll(v, 4, 0))


def join_kernel(part, edge, got_a, got_b, ext, near, far):
    n = part.shape[0]
    parity, has_below, has_above = slab_place()
    x, _ = chip_and_core()
    for i in range(3):
        low = jnp.where(parity == 0, got_b[i], got_a[i])
        high = jnp.where(parity == 0, got_a[i + 1], got_b[i + 1])
        if i == 2:
            low = jnp.where(has_below, low + edge[0], 0.0)
        if i == 0:
            high = jnp.where(has_above, high + edge[1], 0.0)
        ext[i] = low
        ext[n + 3 + i] = high
    for i in range(n):
        v = part[i]
        if i == 0:
            v = v + jnp.where(parity == 0, got_b[3], got_a[3])
        if i == n - 1:
            v = v + jnp.where(parity == 0, got_a[0], got_b[0])
        ext[i + 3] = v
    span = near.shape[1]
    step = ext.shape[1] - span
    near[...] = ext[:, pl.ds(pl.multiple_of(x * step, 8), span), :]
    there = (1 - x) * step

    def layer(i, start, size):
        return ext[i + 2, pl.ds(pl.multiple_of(there + start, 8), size), :]

    pack(far, layer, n + 2, 1 - x, ext.shape[1] // 2)


def warp_kernel(ext, offs, near, far, wide, full):
    n, tall = offs.shape[1], ext.shape[1]
    depth = n + 4
    columns, lanes = wide.shape[1], wide.shape[4]
    blank = jnp.zeros((8, lanes), F32)

    def fill(z, carry):
        v = ext[z + 1]
        for s in range(5):
            moved = v if s == 2 else shift_lanes(v, s - 2)
            for c in range(columns):
                wide[s, c, z, pl.ds(0, 8), :] = blank
                wide[s, c, z, pl.ds(8, tall), :] = moved[:, c * lanes : (c + 1) * lanes]
                wide[s, c, z, pl.ds(8 + tall, 8), :] = blank
        return carry

    lax.fori_loop(0, depth, fill, 0)

    def weights(comp, z, y, c):
        h = offs[comp, z, pl.ds(y, 8), pl.ds(c * lanes, lanes)].astype(F32) * 0.5
        return [jnp.maximum(1.0 - jnp.abs(h - (s - 2.0)), 0.0) for s in range(5)]

    def tile(i, carry):
        z = i // (tall // 8)
        y = pl.multiple_of((i % (tall // 8)) * 8, 8)
        for c in range(columns):
            wz, wy, wx = (weights(m, z, y, c) for m in range(3))
            total = None
            for a in range(5):
                plane = None
                for b in range(5):
                    line = None
                    for s in range(5):
                        term = wx[s] * wide[s, c, z + a, pl.ds(y + 6 + b, 8), :]
                        line = term if line is None else line + term
                    line = wy[b] * line
                    plane = line if plane is None else plane + line
                plane = wz[a] * plane
                total = plane if total is None else total + plane
            full[z, pl.ds(y, 8), pl.ds(c * lanes, lanes)] = total
        return carry

    lax.fori_loop(0, n * (tall // 8), tile, 0)
    x, _ = chip_and_core()
    span = near.shape[1]
    step = tall - span
    near[...] = full[:, pl.ds(pl.multiple_of(x * step, 8), span), :]
    there = (1 - x) * step

    def layer(i, start, size):
        return full[i, pl.ds(pl.multiple_of(there + start, 8), size), :]

    pack(far, layer, n, 1 - x, tall // 2)


def cut_kernel(vel, far, held, sem):
    x, _ = chip_and_core()
    n, tall = vel.shape[1:3]
    span = held.shape[2]
    there = pl.multiple_of((1 - x) * (tall - span), 8)
    copy = pltpu.make_async_copy(vel.at[:, :, pl.ds(there, span), :], held, sem)
    copy.start()
    copy.wait()

    def layer(i, start, size):
        return held[i // n, i % n, pl.ds(start, size), :]

    pack(far, layer, 3 * n, 1 - x, tall // 2)


def rim_own_kernel(vel, buf_a, buf_b, stage, sem):
    x, _ = chip_and_core()
    parity, _, _ = slab_place()
    n = vel.shape[1]
    span = stage.shape[3]
    start = pl.multiple_of(x * (vel.shape[2] - span), 8)
    copies = [
        pltpu.make_async_copy(vel.at[:, pl.ds(z, 2), pl.ds(start, span), :], stage.at[j], sem.at[j])
        for j, z in enumerate((0, n - 2))
    ]
    for copy in copies:
        copy.start()
    for copy in copies:
        copy.wait()
    below, above = stage[0], stage[1]
    buf_a[...] = jnp.where(parity == 0, above, below)
    buf_b[...] = jnp.where(parity == 0, below, above)


def rim_other_kernel(vel_far, diag_far, buf_a, buf_b, vel_other, diag):
    x, _ = chip_and_core()
    parity, _, _ = slab_place()
    n, span = vel_other.shape[1:3]
    half = span - RIM

    def store_vel(i, start, size, v):
        vel_other[i // n, i % n, pl.ds(start, size), :] = v

    def store_diag(i, start, size, v):
        diag[i, pl.ds(start, size), :] = v

    unpack(vel_far, store_vel, 3 * n, x, half)
    unpack(diag_far, store_diag, n + 2, x, half)
    for comp in range(3):
        for i in range(2):
            below, above = vel_other[comp, i], vel_other[comp, n - 2 + i]
            buf_a[2 * comp + i] = jnp.where(parity == 0, above, below)
            buf_b[2 * comp + i] = jnp.where(parity == 0, below, above)
    for i in range(2):
        below, above = diag[2 + i], diag[n - 2 + i]
        buf_a[6 + i] = jnp.where(parity == 0, above, below)
        buf_b[6 + i] = jnp.where(parity == 0, below, above)


def rim_warp_kernel(near, far, buf_a, buf_b, other):
    x, _ = chip_and_core()
    parity, _, _ = slab_place()
    n, span = near.shape[:2]

    def store(i, start, size, v):
        other[i, pl.ds(start, size), :] = v

    unpack(far, store, n, x, span - RIM)
    for m in range(2):
        ref = near if m == 0 else other
        for i in range(2):
            below, above = ref[i], ref[n - 2 + i]
            buf_a[m, i] = jnp.where(parity == 0, above, below)
            buf_b[m, i] = jnp.where(parity == 0, below, above)


def pick(parity, got_a, got_b, high):
    a, b = (got_a, got_b) if high else (got_b, got_a)
    return jnp.where(parity == 0, a, b)


def update(velocity, warped, low, here, high, valid):
    gz = (high - low) * 0.5
    gy = (shift_rows(here, True) - shift_rows(here, False)) * 0.5
    gx = (shift_lanes(here, 1) - shift_lanes(here, -1)) * 0.5
    mismatch = warped + velocity[0] * gz + velocity[1] * gy + velocity[2] * gx - here
    denominator = (gz * gz + gy * gy + gx * gx) + mismatch * mismatch + 1.0
    ratio = mismatch / denominator
    after = [v - ratio * g for v, g in zip(velocity, (gz, gy, gx))]
    return after if valid is None else [jnp.where(valid, v, 0.0) for v in after]


def smooth_plane(v):
    v = (shift_rows(v, False) + 2.0 * v + shift_rows(v, True)) * 0.25
    return (shift_lanes(v, -1) + 2.0 * v + shift_lanes(v, 1)) * 0.25


def blur(parts, rows=None):
    low, here, high = parts
    v = smooth_plane((low + 2.0 * here + high) * 0.25)
    if rows is None:
        return v
    x, half = rows
    return jnp.where(x == 0, v[:half], v[v.shape[0] - half :])


def first_mid_kernel(
    vel, vel_other, warp, warp_other, chip, diag, moved, out, out_sum, targets
):
    x, core = chip_and_core()
    n, span = vel_other.shape[1], vel_other.shape[2]
    start = pl.multiple_of(x * (vel.shape[2] - span), 8)
    for i in range(n + 2):
        a, b = chip[i + 2], diag[i]
        targets[0, i] = jnp.where(core == 0, a, b)
        targets[1, i] = jnp.where(core == 0, b, a)

    def step(i, carry):
        for m in range(2):
            if m == 0:
                v = [vel[comp, i, pl.ds(start, span), :] for comp in range(3)]
            else:
                v = [vel_other[comp, i] for comp in range(3)]
            base = warp[i] if m == 0 else warp_other[i]
            v = update(v, base, targets[m, i], targets[m, i + 1], targets[m, i + 2], None)
            for comp in range(3):
                moved[m, comp, i] = v[comp]
        return carry

    lax.fori_loop(0, n, step, 0)

    def smooth(i, carry):
        for comp in range(3):
            both = [blur([moved[m, comp, i + k] for k in range(3)]) for m in range(2)]
            for m in range(2):
                out[m, comp, i] = both[m]
            out_sum[comp, i] = both[0] + both[1]
        return carry

    lax.fori_loop(0, n - 2, smooth, 0)


def first_rim_kernel(
    own_a, own_b, rim_a, rim_b, warp_a, warp_b, chip, diag, mid,
    out, out_sum, targets, held, base, moved,
):
    _, core = chip_and_core()
    parity, has_below, has_above = slab_place()
    n = mid.shape[2]
    for k in range(5):
        low = pick(parity, rim_a[6 + k], rim_b[6 + k], False) if k < 2 else diag[k - 2]
        high = pick(parity, rim_a[3 + k], rim_b[3 + k], True) if k > 2 else diag[n - 1 + k]
        for side, b in enumerate((low, high)):
            a = chip[(n + 1) * side + k]
            targets[side, 0, k] = jnp.where(core == 0, a, b)
            targets[side, 1, k] = jnp.where(core == 0, b, a)
    for m in range(2):
        for side in range(2):
            for r in range(2):
                e = 2 * side + r
                base[m, e] = pick(parity, warp_a[m, r], warp_b[m, r], side == 1)
                for comp in range(3):
                    if m == 0:
                        a, b = own_a[comp, r], own_b[comp, r]
                    else:
                        a, b = rim_a[2 * comp + r], rim_b[2 * comp + r]
                    held[m, comp, e] = pick(parity, a, b, side == 1)
                    moved[side, m, comp, r + 2 * (1 - side)] = mid[m, comp, (n - 2) * side + r]

    def step(j, carry):
        m, e = j // 4, j % 4
        side, r = e // 2, e % 2
        at = side + r
        v = update(
            [held[m, comp, e] for comp in range(3)], base[m, e],
            targets[side, m, at], targets[side, m, at + 1], targets[side, m, at + 2],
            jnp.where(side == 0, has_below, has_above),
        )
        for comp in range(3):
            moved[side, m, comp, e] = v[comp]
        return carry

    lax.fori_loop(0, 8, step, 0)

    def smooth(e, carry):
        side, r = e // 2, e % 2
        valid = (side == r) & jnp.where(side == 0, has_below, has_above) | (side != r)
        for comp in range(3):
            both = [blur([moved[side, m, comp, r + k] for k in range(3)]) for m in range(2)]
            for m in range(2):
                both[m] = jnp.where(valid, both[m], 0.0)
                out[m, comp, e] = both[m]
            out_sum[comp, e] = both[0] + both[1]
        return carry

    lax.fori_loop(0, 4, smooth, 0)


def second_mid_kernel(vel, beside, warp, warp_other, targets, moved, out, out_sum):
    x, _ = chip_and_core()
    inner, half = vel.shape[2], out.shape[3]

    def step(i, carry):
        for m in range(2):
            v = [(2.0 * vel[m, comp, i] + beside[comp, i]) * 0.25 for comp in range(3)]
            base = warp[i + 1] if m == 0 else warp_other[i + 1]
            v = update(v, base, targets[m, i + 1], targets[m, i + 2], targets[m, i + 3], None)
            for comp in range(3):
                moved[m, comp, i] = v[comp]
        return carry

    lax.fori_loop(0, inner, step, 0)

    def smooth(i, carry):
        for comp in range(3):
            both = [blur([moved[m, comp, i + k] for k in range(3)], (x, half)) for m in range(2)]
            for m in range(2):
                out[m, comp, i] = both[m]
            out_sum[comp, i] = both[0] + both[1]
        return carry

    lax.fori_loop(0, inner - 2, smooth, 0)


def second_rim_kernel(
    vel, beside, warp, warp_other, warp_a, warp_b, mid, targets, out, out_sum, base, moved
):
    x, _ = chip_and_core()
    parity, has_below, has_above = slab_place()
    inner, half = mid.shape[2], out.shape[3]
    n = inner + 2
    for m in range(2):
        own = warp if m == 0 else warp_other
        base[m, 0] = pick(parity, warp_a[m, 1], warp_b[m, 1], False)
        base[m, 1] = own[0]
        base[m, 2] = own[n - 1]
        base[m, 3] = pick(parity, warp_a[m, 0], warp_b[m, 0], True)
        for comp in range(3):
            for r in range(2):
                moved[0, m, comp, 2 + r] = mid[m, comp, r]
                moved[1, m, comp, r] = mid[m, comp, inner - 2 + r]

    def step(j, carry):
        m, e = j // 4, j % 4
        side, r = e // 2, e % 2
        at = 1 - side + r
        valid = (side == r) & jnp.where(side == 0, has_below, has_above) | (side != r)
        v = update(
            [(2.0 * vel[m, comp, e] + beside[comp, e]) * 0.25 for comp in range(3)], base[m, e],
            targets[side, m, at], targets[side, m, at + 1], targets[side, m, at + 2], valid,
        )
        for comp in range(3):
            moved[side, m, comp, e] = v[comp]
        return carry

    lax.fori_loop(0, 8, step, 0)

    def smooth(e, carry):
        side, r = e // 2, e % 2
        for comp in range(3):
            both = [
                blur([moved[side, m, comp, r + k] for k in range(3)], (x, half)) for m in range(2)
            ]
            for m in range(2):
                out[m, comp, e] = both[m]
            out_sum[comp, e] = both[0] + both[1]
        return carry

    lax.fori_loop(0, 4, smooth, 0)


def send_kernel(vel, beside, out):
    out[...] = (2.0 * vel[1] + beside[...]) * 0.25


def close_own_kernel(mid, mid_beside, rim, rim_beside, out, stage_mid, stage_rim, sem):
    x, _ = chip_and_core()
    half = stage_mid.shape[2]
    rows = pl.ds(pl.multiple_of(x * half, 8), half)
    n = out.shape[1]
    stage_mid[...] = (2.0 * mid[0] + mid_beside[...]) * 0.25
    stage_rim[...] = (2.0 * rim[0] + rim_beside[...]) * 0.25
    copies = [
        pltpu.make_async_copy(stage_mid, out.at[:, pl.ds(2, n - 4), rows, :], sem.at[0]),
        pltpu.make_async_copy(stage_rim.at[:, pl.ds(0, 2)], out.at[:, pl.ds(0, 2), rows, :], sem.at[1]),
        pltpu.make_async_copy(stage_rim.at[:, pl.ds(2, 2)], out.at[:, pl.ds(n - 2, 2), rows, :], sem.at[2]),
    ]
    for copy in copies:
        copy.start()
    for copy in copies:
        copy.wait()


def close_mid_kernel(done, home, out, sem):
    del done
    x, _ = chip_and_core()
    half = home.shape[2]
    rows = pl.ds(pl.multiple_of((1 - x) * half, 8), half)
    copy = pltpu.make_async_copy(home, out.at[:, pl.ds(2, out.shape[1] - 4), rows, :], sem)
    copy.start()
    copy.wait()


def close_rim_kernel(done, home, out, sem):
    del done
    x, _ = chip_and_core()
    half = home.shape[2]
    rows = pl.ds(pl.multiple_of((1 - x) * half, 8), half)
    copies = [
        pltpu.make_async_copy(
            home.at[:, pl.ds(2 * k, 2)], out.at[:, pl.ds(z, 2), rows, :], sem.at[k]
        )
        for k, z in enumerate((0, out.shape[1] - 2))
    ]
    for copy in copies:
        copy.start()
    for copy in copies:
        copy.wait()


def swaps(count, first):
    pairs = []
    for i in range(first, count - 1, 2):
        pairs += [(i, i + 1), (i + 1, i)]
    return pairs


def swap_slabs(buf_a, buf_b):
    count = lax.axis_size("slab")
    got_a = lax.ppermute(buf_a, "slab", swaps(count, 0))
    got_b = lax.ppermute(buf_b, "slab", swaps(count, 1))
    return got_a, got_b


def swap_phases(values, mask):
    return lax.ppermute(values, "phase", [(i, i ^ mask) for i in range(lax.axis_size("phase"))])


def ring_of_four(fine_images, offsets, velocity_init):
    return four_phases(fine_images, offsets, velocity_init)


def four_phases(fine_images, offsets, velocity_init):
    fine, offs, vel = fine_images[0], offsets[0], velocity_init[0]
    deep, tall, wide = fine.shape
    n, rows, cols = offs.shape[1:]
    half = rows // 2
    span = half + RIM
    lanes = 128
    dma = pltpu.SemaphoreType.DMA

    (vel_cut,) = launch(
        cut_kernel,
        [shape(3 * n * (half + 4), cols)],
        [vel],
        [pltpu.VMEM((3, n, span, cols), F32), dma],
        hbm=(0,),
        micros=1.0,
    )
    vel_far = swap_phases(vel_cut, 2)

    part, edge, buf_a, buf_b = launch(
        halve_kernel,
        [shape(n, rows, cols), shape(2, rows, cols), shape(4, rows, cols), shape(4, rows, cols)],
        [fine],
        [
            pltpu.VMEM((deep, tall, wide), F32),
            pltpu.VMEM((wide, cols), BF16),
            pltpu.VMEM((cols // lanes, 2 * tall, lanes), F32),
            pltpu.VMEM((rows, cols), F32),
            dma((n,)),
        ],
        hbm=(0,),
        micros=4.0,
    )
    got_a, got_b = swap_slabs(buf_a, buf_b)
    buf_a, buf_b = launch(
        rim_own_kernel,
        [shape(3, 2, span, cols)] * 2,
        [vel],
        [pltpu.VMEM((2, 3, 2, span, cols), F32), dma((2,))],
        hbm=(0,),
    )
    own_a, own_b = swap_slabs(buf_a, buf_b)
    ext, near, far = launch(
        join_kernel,
        [shape(n + 6, rows, cols), shape(n + 6, span, cols), shape((n + 2) * (half + 4), cols)],
        [part, edge, got_a, got_b],
    )
    chip = swap_phases(near, 1)
    diag_far = swap_phases(far, 3)

    warp, warp_cut = launch(
        warp_kernel,
        [shape(n, span, cols), shape(n * (half + 4), cols)],
        [ext, offs],
        [
            pltpu.VMEM((5, cols // lanes, n + 4, rows + 16, lanes), F32),
            pltpu.VMEM((n, rows, cols), F32),
        ],
        micros=8.5,
    )
    warp_far = swap_phases(warp_cut, 2)

    buf_a, buf_b, vel_other, diag = launch(
        rim_other_kernel,
        [shape(8, span, cols)] * 2 + [shape(3, n, span, cols), shape(n + 2, span, cols)],
        [vel_far, diag_far],
    )
    rim_a, rim_b = swap_slabs(buf_a, buf_b)
    buf_a, buf_b, warp_other = launch(
        rim_warp_kernel,
        [shape(2, 2, span, cols)] * 2 + [shape(n, span, cols)],
        [warp, warp_far],
    )
    warp_a, warp_b = swap_slabs(buf_a, buf_b)

    moved, mid, mid_sum, targets = launch(
        first_mid_kernel,
        [
            shape(2, 3, n, span, cols),
            shape(2, 3, n - 2, span, cols),
            shape(3, n - 2, span, cols),
            shape(2, n + 2, span, cols),
        ],
        [vel, vel_other, warp, warp_other, chip, diag],
        micros=3.3,
    )
    mid_beside = swap_phases(mid_sum, 1)
    rim, rim_sum, ends = launch(
        first_rim_kernel,
        [shape(2, 3, 4, span, cols), shape(3, 4, span, cols), shape(2, 2, 5, span, cols)],
        [own_a, own_b, rim_a, rim_b, warp_a, warp_b, chip, diag, moved],
        [
            pltpu.VMEM((2, 3, 4, span, cols), F32),
            pltpu.VMEM((2, 4, span, cols), F32),
            pltpu.VMEM((2, 2, 3, 4, span, cols), F32),
        ],
        micros=2.0,
    )
    rim_beside = swap_phases(rim_sum, 1)
    moved, mid, mid_sum = launch(
        second_mid_kernel,
        [
            shape(2, 3, n - 2, span, cols),
            shape(2, 3, n - 4, half, cols),
            shape(3, n - 4, half, cols),
        ],
        [mid, mid_beside, warp, warp_other, targets],
        micros=2.5,
    )
    mid_beside = swap_phases(mid_sum, 1)
    rim, rim_sum = launch(
        second_rim_kernel,
        [shape(2, 3, 4, half, cols), shape(3, 4, half, cols)],
        [rim, rim_beside, warp, warp_other, warp_a, warp_b, moved, ends],
        [
            pltpu.VMEM((2, 4, span, cols), F32),
            pltpu.VMEM((2, 2, 3, 4, span, cols), F32),
        ],
        micros=2.0,
    )
    rim_beside = swap_phases(rim_sum, 1)
    (away,) = launch(send_kernel, [shape(3, n - 4, half, cols)], [mid, mid_beside])
    mid_home = swap_phases(away, 2)
    (away,) = launch(send_kernel, [shape(3, 4, half, cols)], [rim, rim_beside])
    rim_home = swap_phases(away, 2)
    (velocity,) = launch(
        close_own_kernel,
        [shape(3, n, rows, cols)],
        [mid, mid_beside, rim, rim_beside],
        [
            pltpu.VMEM((3, n - 4, half, cols), F32),
            pltpu.VMEM((3, 4, half, cols), F32),
            dma((3,)),
        ],
        hbm_out=(0,),
    )
    for kernel, home, sems in ((close_mid_kernel, mid_home, dma), (close_rim_kernel, rim_home, dma((2,)))):
        (velocity,) = launch(
            kernel,
            [shape(3, n, rows, cols)],
            [velocity, home],
            [sems],
            hbm=(0,),
            hbm_out=(0,),
            alias={0: 0},
        )
    return velocity[None]


highest = lax.Precision.HIGHEST


def extended(cells, sides, width):
    for axis, dim in sides:
        count = lax.axis_size(axis)
        ends = count - 1
        head = lax.slice_in_dim(cells, 0, width, axis=dim)
        tail = lax.slice_in_dim(cells, cells.shape[dim] - width, cells.shape[dim], axis=dim)
        cells = jnp.concatenate(
            [
                lax.ppermute(tail, axis, [(i, (i + 1) % count) for i in range(ends)]),
                cells,
                lax.ppermute(head, axis, [((i + 1) % count, i) for i in range(ends)]),
            ],
            axis=dim,
        )
    return cells


def passed_along(block, axis, distance):
    devices = range(lax.axis_size(axis))
    route = [((i - distance) % len(devices), i) for i in devices]
    return lax.ppermute(block, axis, route)


def pad_axis(values, dimension, width):
    widths = [(0, 0)] * values.ndim
    widths[dimension] = (width, width)
    return jnp.pad(values, widths)


def halve_matrix(length):
    fine_index = lax.broadcasted_iota(jnp.int32, (length, length // 2), 0)
    coarse_index = lax.broadcasted_iota(jnp.int32, (length, length // 2), 1)
    outer = (fine_index == 2 * coarse_index - 1) | (fine_index == 2 * coarse_index + 2)
    inner = (fine_index == 2 * coarse_index) | (fine_index == 2 * coarse_index + 1)
    return jnp.where(inner, 0.375, jnp.where(outer, 0.125, 0.0)).astype(jnp.float32)


def smooth_matrix(length):
    source = lax.broadcasted_iota(jnp.int32, (length, length), 0)
    result = lax.broadcasted_iota(jnp.int32, (length, length), 1)
    return jnp.where(
        source == result, 0.5, jnp.where(jnp.abs(source - result) == 1, 0.25, 0.0)
    ).astype(jnp.float32)


def gradient_matrix(length):
    source = lax.broadcasted_iota(jnp.int32, (length, length), 0)
    result = lax.broadcasted_iota(jnp.int32, (length, length), 1)
    return jnp.where(source == result + 1, 0.5, jnp.where(source == result - 1, -0.5, 0.0)).astype(
        jnp.float32
    )


def along_last(values, matrix):
    return jnp.einsum("...j,jk->...k", values, matrix, precision=highest)


def along_rows(values, matrix):
    return jnp.einsum("...jx,jk->...kx", values, matrix, precision=highest)


def halve_depth(values):
    count, depth = (values.shape[0], values.shape[1])
    pairs = values.reshape((count, depth // 2, 2) + values.shape[2:])
    even = pairs[:, :, 0]
    odd = pairs[:, :, 1]
    return (even[:, :-1] + 3.0 * odd[:, :-1] + 3.0 * even[:, 1:] + odd[:, 1:]) * 0.125


def depth_gradient(values):
    length = values.shape[1] - 2
    return (values[:, 2 : 2 + length] - values[:, 0:length]) * 0.5


def depth_smooth(values):
    length = values.shape[2] - 2
    return (
        values[:, :, 0:length] + 2.0 * values[:, :, 1 : 1 + length] + values[:, :, 2 : 2 + length]
    ) * 0.25


def axis_weights(offsets):
    return [
        jnp.where(
            2 * displace == offsets, 1.0, jnp.where(jnp.abs(2 * displace - offsets) == 1, 0.5, 0.0)
        ).astype(jnp.float32)
        for displace in range(-2, 3)
    ]


def warp_moving(moving_rows, offsets):
    layers, height, breadth = (offsets.shape[2], offsets.shape[3], offsets.shape[4])
    weights_z = axis_weights(offsets[:, 0])
    weights_y = axis_weights(offsets[:, 1])
    weights_x = axis_weights(offsets[:, 2])
    shape = offsets[:, 0].shape
    rows_padded = pad_axis(moving_rows, 2, 2)
    wide = pad_axis(rows_padded, 3, 2)
    shifted = [wide[..., index_x : index_x + breadth] for index_x in range(5)]
    warped = jnp.zeros(shape, jnp.float32)
    for index_z in range(5):
        plane_sum = jnp.zeros(shape, jnp.float32)
        for index_y in range(5):
            line_sum = jnp.zeros(shape, jnp.float32)
            for index_x in range(5):
                window = shifted[index_x][:, index_z : index_z + layers, index_y : index_y + height]
                line_sum = line_sum + weights_x[index_x] * window
            plane_sum = plane_sum + weights_y[index_y] * line_sum
        warped = warped + weights_z[index_z] * plane_sum
    return warped


def shards(fine_images, offsets, velocity_init):
    fine_height, fine_breadth = (fine_images.shape[2], fine_images.shape[3])
    rimmed_fine = extended(fine_images, (("slab", 1),), 1)
    coarse = halve_depth(rimmed_fine)
    coarse = along_rows(coarse, halve_matrix(fine_height))
    coarse = along_last(coarse, halve_matrix(fine_breadth))
    target = passed_along(coarse, "phase", -1)
    height, breadth = (coarse.shape[2], coarse.shape[3])
    moving_rows = extended(coarse, (("slab", 1),), 2)
    target_rows = extended(target, (("slab", 1),), 1)
    grad_z = depth_gradient(target_rows)
    grad_y = along_rows(target, gradient_matrix(height))
    grad_x = along_last(target, gradient_matrix(breadth))
    gradients = jnp.stack([grad_z, grad_y, grad_x], axis=1)
    norm_squared = grad_z * grad_z + grad_y * grad_y + grad_x * grad_x
    warped_base = warp_moving(moving_rows, offsets)
    smooth_rows = smooth_matrix(height)
    smooth_columns = smooth_matrix(breadth)
    velocity = velocity_init
    for _ in range(ITERS):
        warped = (
            warped_base
            + velocity[:, 0] * grad_z
            + velocity[:, 1] * grad_y
            + velocity[:, 2] * grad_x
        )
        mismatch = warped - target
        denominator = norm_squared + mismatch * mismatch + 1.0
        velocity = velocity - (mismatch / denominator)[:, None] * gradients
        rimmed = extended(velocity, (("slab", 2),), 1)
        velocity = depth_smooth(rimmed)
        velocity = along_rows(velocity, smooth_rows)
        velocity = along_last(velocity, smooth_columns)
        earlier = passed_along(velocity, "phase", 1)
        later = passed_along(velocity, "phase", -1)
        velocity = (earlier + 2.0 * velocity + later) * 0.25
    return velocity


def solution(mesh):
    placed = (
        P(("case", "phase"), "slab", None, None),
        P(("case", "phase"), None, "slab", None, None),
        P(("case", "phase"), None, "slab", None, None),
    )
    four = mesh.shape["phase"] == 4
    return jax.shard_map(
        ring_of_four if four else shards,
        mesh=mesh,
        in_specs=placed,
        out_specs=P(("case", "phase"), None, "slab", None, None),
        check_vma=False,
    )
```

```python
import jax
import jax.numpy as jnp
from jax import lax
from jax.experimental import pallas as pl
from jax.experimental.pallas import tpu as pltpu
from jax.sharding import PartitionSpec as P


ITERS = 2
RIM = 8
F32 = jnp.float32
BF16 = jnp.bfloat16


def launch(body, outs, ins, scratch=(), hbm=(), hbm_out=(), micros=1.0, limit=16, alias={}):
    spaces = [pltpu.HBM if i in hbm else pltpu.VMEM for i in range(len(ins))]
    targets = [pl.ANY if i in hbm_out else pltpu.VMEM for i in range(len(outs))]
    return pl.pallas_call(
        body,
        out_shape=outs,
        in_specs=[pl.BlockSpec(memory_space=space) for space in spaces],
        out_specs=[pl.BlockSpec(memory_space=space) for space in targets],
        scratch_shapes=scratch,
        input_output_aliases=alias,
        compiler_params=pltpu.CompilerParams(vmem_limit_bytes=limit * 2**20),
        cost_estimate=pl.CostEstimate(
            flops=0, bytes_accessed=int(micros * 3.3e6), transcendentals=0
        ),
    )(*[pltpu.with_memory_space_constraint(v, pltpu.HBM) if i in hbm and i not in alias else v for i, v in enumerate(ins)])


def shape(*dims):
    return jax.ShapeDtypeStruct(dims, F32)


def chip_and_core():
    phase = lax.axis_index("phase")
    return phase // 2, phase % 2


def slab_place():
    slab = lax.axis_index("slab")
    last = lax.axis_size("slab") - 1
    return slab % 2, slab > 0, slab < last


def shift_rows(a, up):
    zero = jnp.zeros((1, a.shape[1]), a.dtype)
    return jnp.concatenate([a[1:], zero], 0) if up else jnp.concatenate([zero, a[:-1]], 0)


def shift_lanes(a, step):
    lanes = 128
    count = a.shape[1] // lanes
    lane = lax.broadcasted_iota(jnp.int32, (a.shape[0], lanes), 1)
    turned = [pltpu.roll(a[:, c * lanes : (c + 1) * lanes], (-step) % lanes, 1) for c in range(count)]
    edge = lane >= lanes - step if step > 0 else lane < -step
    ahead = 1 if step > 0 else -1
    cols = []
    for c in range(count):
        beyond = turned[c + ahead] if 0 <= c + ahead < count else 0.0
        cols.append(jnp.where(edge, beyond, turned[c]))
    return jnp.concatenate(cols, 1)


def halve_kernel(fine, part, edge, buf_a, buf_b, held, mat, rows, prev, sems):
    count, tall, wide = fine.shape
    n, half = count // 2, tall // 2
    cut = rows.shape[2]

    def fetch(k):
        pair = pl.ds(2 * k, 2)
        return pltpu.make_async_copy(fine.at[pair], held.at[pair], sems.at[k])

    for k in range(n):
        fetch(k).start()
    i = lax.broadcasted_iota(jnp.int32, mat.shape, 0)
    j = lax.broadcasted_iota(jnp.int32, mat.shape, 1)
    d = i - 2 * j
    inner = (d == 0) | (d == 1)
    outer = (d == -1) | (d == 2)
    mat[...] = jnp.where(inner, 0.375, jnp.where(outer, 0.125, 0.0)).astype(BF16)

    def pair(k, carry):
        fetch(k).wait()
        f = held[pl.ds(2 * k, 2)].reshape(2 * tall, wide)
        hi = f.astype(BF16)
        lo = (f - hi.astype(F32)).astype(BF16)
        w = mat[...]
        got = jnp.dot(hi, w, preferred_element_type=F32)
        got += jnp.dot(lo, w, preferred_element_type=F32)
        for c in range(rows.shape[0]):
            rows[c] = got[:, c * cut : (c + 1) * cut]
        layers = []
        for z in range(2):
            cols = []
            for c in range(rows.shape[0]):
                even = rows[c, pl.ds(z * tall, half, 2), :]
                odd = rows[c, pl.ds(z * tall + 1, half, 2), :]
                cols.append(
                    (shift_rows(odd, False) + shift_rows(even, True) + 3.0 * (even + odd))
                    * (1.0 / 64.0)
                )
            layers.append(jnp.concatenate(cols, 1))
        even, odd = layers
        mid = 3.0 * (even + odd)

        @pl.when(k == 0)
        def _():
            edge[0] = even
            part[0] = mid

        @pl.when(k > 0)
        def _():
            part[k] = mid + prev[...]
            part[k - 1] += even

        prev[...] = odd
        return carry

    lax.fori_loop(0, n, pair, 0)
    edge[1] = prev[...]
    parity, _, _ = slab_place()
    for i in range(4):
        above = edge[1] if i == 3 else part[n - 3 + i]
        below = edge[0] if i == 0 else part[i - 1]
        buf_a[i] = jnp.where(parity == 0, above, below)
        buf_b[i] = jnp.where(parity == 0, below, above)


def slots(keep, chip, cols):
    group = 8 // keep
    slot = lax.broadcasted_iota(jnp.int32, (8, cols), 0) // keep
    return jnp.where(chip == 0, slot, (slot + 1) % group)


def pack(dst, layer, count, chip, half, keep):
    which = slots(keep, chip, dst.shape[1])
    main = pl.multiple_of(8 * chip, 8)
    rim = pl.multiple_of(half * (1 - chip), 8)
    group = 8 // keep
    for i in range(count):
        dst[pl.ds(i * half, half), :] = layer(i, main, half)
    for i in range(0, count, group):
        tile = layer(i, rim, 8)
        for g in range(1, group):
            tile = jnp.where(which == g, pltpu.roll(layer(i + g, rim, 8), keep * g, 0), tile)
        dst[pl.ds(count * half + keep * i, 8), :] = tile


def unpack(src, store, count, chip, half, keep):
    main = pl.multiple_of(8 * chip, 8)
    rim = pl.multiple_of(half * (1 - chip), 8)
    group = 8 // keep
    for i in range(count):
        store(i, main, half, src[pl.ds(i * half, half), :])
    for i in range(0, count, group):
        v = src[pl.ds(count * half + keep * i, 8), :]
        for g in range(group):
            store(i + g, rim, 8, v if g == 0 else pltpu.roll(v, 8 - keep * g, 0))


def join_kernel(part, edge, got_a, got_b, ext, near, far):
    n = part.shape[0]
    parity, has_below, has_above = slab_place()
    x, _ = chip_and_core()
    for i in range(3):
        low = jnp.where(parity == 0, got_b[i], got_a[i])
        high = jnp.where(parity == 0, got_a[i + 1], got_b[i + 1])
        if i == 2:
            low = jnp.where(has_below, low + edge[0], 0.0)
        if i == 0:
            high = jnp.where(has_above, high + edge[1], 0.0)
        ext[i] = low
        ext[n + 3 + i] = high
    for i in range(n):
        v = part[i]
        if i == 0:
            v = v + jnp.where(parity == 0, got_b[3], got_a[3])
        if i == n - 1:
            v = v + jnp.where(parity == 0, got_a[0], got_b[0])
        ext[i + 3] = v
    span = near.shape[1]
    step = ext.shape[1] - span
    near[...] = ext[:, pl.ds(pl.multiple_of(x * step, 8), span), :]
    there = (1 - x) * step

    def layer(i, start, size):
        return ext[i + 2, pl.ds(pl.multiple_of(there + start, 8), size), :]

    pack(far, layer, n + 2, 1 - x, ext.shape[1] // 2, 4)


def warp_kernel(ext, offs, near, far, wide, full):
    n, tall = offs.shape[1], ext.shape[1]
    depth = n + 4
    columns, lanes = wide.shape[1], wide.shape[4]
    blank = jnp.zeros((8, lanes), F32)

    def fill(z, carry):
        v = ext[z + 1]
        whole = [v if k == 0 else shift_lanes(v, k) for k in range(-2, 3)]
        for k in range(5):
            moved = whole[0] if k == 0 else whole[k] - whole[k - 1]
            for c in range(columns):
                wide[k, c, z, pl.ds(0, 8), :] = blank
                wide[k, c, z, pl.ds(8, tall), :] = moved[:, c * lanes : (c + 1) * lanes]
                wide[k, c, z, pl.ds(8 + tall, 8), :] = blank
        return carry

    lax.fori_loop(0, depth, fill, 0)

    def shares(comp, z, y, c):
        h = offs[comp, z, pl.ds(y, 8), pl.ds(c * lanes, lanes)].astype(F32) * 0.5
        return [jnp.minimum(jnp.maximum(h - k, 0.0), 1.0) for k in range(-2, 2)]

    def weights(comp, z, y, c):
        s = shares(comp, z, y, c)
        return [1.0 - s[0], s[0] - s[1], s[1] - s[2], s[2] - s[3], s[3]]

    def tile(i, carry):
        z = i // (tall // 8)
        y = pl.multiple_of((i % (tall // 8)) * 8, 8)
        for c in range(columns):
            wz, wy = weights(0, z, y, c), weights(1, z, y, c)
            sx = shares(2, z, y, c)
            total = None
            for a in range(5):
                plane = None
                for b in range(5):
                    line = wide[0, c, z + a, pl.ds(y + 6 + b, 8), :]
                    for k in range(4):
                        line += sx[k] * wide[k + 1, c, z + a, pl.ds(y + 6 + b, 8), :]
                    line = wy[b] * line
                    plane = line if plane is None else plane + line
                plane = wz[a] * plane
                total = plane if total is None else total + plane
            full[z, pl.ds(y, 8), pl.ds(c * lanes, lanes)] = total
        return carry

    lax.fori_loop(0, n * (tall // 8), tile, 0)
    x, _ = chip_and_core()
    span = near.shape[1]
    step = tall - span
    near[...] = full[:, pl.ds(pl.multiple_of(x * step, 8), span), :]
    there = (1 - x) * step

    def layer(i, start, size):
        return full[i, pl.ds(pl.multiple_of(there + start, 8), size), :]

    pack(far, layer, n, 1 - x, tall // 2, 2)


def cut_kernel(vel, far, held, sem):
    x, _ = chip_and_core()
    n, tall = vel.shape[1:3]
    span = held.shape[2]
    there = pl.multiple_of((1 - x) * (tall - span), 8)
    copy = pltpu.make_async_copy(vel.at[:, :, pl.ds(there, span), :], held, sem)
    copy.start()
    copy.wait()

    def layer(i, start, size):
        return held[i // n, i % n, pl.ds(start, size), :]

    pack(far, layer, 3 * n, 1 - x, tall // 2, 2)


def rim_own_kernel(vel, buf_a, buf_b, stage, sem):
    x, _ = chip_and_core()
    parity, _, _ = slab_place()
    n = vel.shape[1]
    span = stage.shape[3]
    start = pl.multiple_of(x * (vel.shape[2] - span), 8)
    copies = [
        pltpu.make_async_copy(vel.at[:, pl.ds(z, 2), pl.ds(start, span), :], stage.at[j], sem.at[j])
        for j, z in enumerate((0, n - 2))
    ]
    for copy in copies:
        copy.start()
    for copy in copies:
        copy.wait()
    below, above = stage[0], stage[1]
    buf_a[...] = jnp.where(parity == 0, above, below)
    buf_b[...] = jnp.where(parity == 0, below, above)


def rim_other_kernel(vel_far, diag_far, buf_a, buf_b, vel_other, diag):
    x, _ = chip_and_core()
    parity, _, _ = slab_place()
    n, span = vel_other.shape[1:3]
    half = span - RIM

    def store_vel(i, start, size, v):
        vel_other[i // n, i % n, pl.ds(start, size), :] = v

    def store_diag(i, start, size, v):
        diag[i, pl.ds(start, size), :] = v

    unpack(vel_far, store_vel, 3 * n, x, half, 2)
    unpack(diag_far, store_diag, n + 2, x, half, 4)
    for comp in range(3):
        for i in range(2):
            below, above = vel_other[comp, i], vel_other[comp, n - 2 + i]
            buf_a[2 * comp + i] = jnp.where(parity == 0, above, below)
            buf_b[2 * comp + i] = jnp.where(parity == 0, below, above)
    for i in range(2):
        below, above = diag[2 + i], diag[n - 2 + i]
        buf_a[6 + i] = jnp.where(parity == 0, above, below)
        buf_b[6 + i] = jnp.where(parity == 0, below, above)


def rim_warp_kernel(near, far, buf_a, buf_b, other):
    x, _ = chip_and_core()
    parity, _, _ = slab_place()
    n, span = near.shape[:2]

    def store(i, start, size, v):
        other[i, pl.ds(start, size), :] = v

    unpack(far, store, n, x, span - RIM, 2)
    for m in range(2):
        ref = near if m == 0 else other
        for i in range(2):
            below, above = ref[i], ref[n - 2 + i]
            buf_a[m, i] = jnp.where(parity == 0, above, below)
            buf_b[m, i] = jnp.where(parity == 0, below, above)


def pick(parity, got_a, got_b, high):
    a, b = (got_a, got_b) if high else (got_b, got_a)
    return jnp.where(parity == 0, a, b)


def update(velocity, warped, low, here, high, valid):
    gz = (high - low) * 0.5
    gy = (shift_rows(here, True) - shift_rows(here, False)) * 0.5
    gx = (shift_lanes(here, 1) - shift_lanes(here, -1)) * 0.5
    mismatch = warped + velocity[0] * gz + velocity[1] * gy + velocity[2] * gx - here
    denominator = (gz * gz + gy * gy + gx * gx) + mismatch * mismatch + 1.0
    ratio = mismatch / denominator
    after = [v - ratio * g for v, g in zip(velocity, (gz, gy, gx))]
    return after if valid is None else [jnp.where(valid, v, 0.0) for v in after]


def smooth_plane(v):
    v = shift_rows(v, False) + (v + v) + shift_rows(v, True)
    return shift_lanes(v, -1) + (v + v) + shift_lanes(v, 1)


def blur(parts, rows=None):
    low, here, high = parts
    v = smooth_plane((low + (here + here) + high) * (1.0 / 64.0))
    if rows is None:
        return v
    x, half = rows
    return jnp.where(x == 0, v[:half], v[v.shape[0] - half :])


def first_own_kernel(vel, warp, chip, diag, moved, targets):
    x, core = chip_and_core()
    n, span = warp.shape[:2]
    start = pl.multiple_of(x * (vel.shape[2] - span), 8)
    for i in range(n + 2):
        a, b = chip[i + 2], diag[i]
        targets[0, i] = jnp.where(core == 0, a, b)
        targets[1, i] = jnp.where(core == 0, b, a)

    def step(i, carry):
        v = [vel[comp, i, pl.ds(start, span), :] for comp in range(3)]
        v = update(v, warp[i], targets[0, i], targets[0, i + 1], targets[0, i + 2], None)
        for comp in range(3):
            moved[comp, i] = v[comp]
        return carry

    lax.fori_loop(0, n, step, 0)


def first_mid_kernel(vel_other, warp_other, moved_own, targets, moved, out, out_sum):
    n = vel_other.shape[1]

    def step(i, carry):
        v = [vel_other[comp, i] for comp in range(3)]
        v = update(v, warp_other[i], targets[1, i], targets[1, i + 1], targets[1, i + 2], None)
        for comp in range(3):
            moved[comp, i] = v[comp]
        return carry

    lax.fori_loop(0, n, step, 0)

    def smooth(i, carry):
        for comp in range(3):
            both = [blur([ref[comp, i + k] for k in range(3)]) for ref in (moved_own, moved)]
            for m in range(2):
                out[m, comp, i] = both[m]
            out_sum[comp, i] = both[0] + both[1]
        return carry

    lax.fori_loop(0, n - 2, smooth, 0)


def first_rim_kernel(
    own_a, own_b, rim_a, rim_b, warp_a, warp_b, chip, diag, mid_own, mid_other,
    out, out_sum, targets, held, base, moved,
):
    _, core = chip_and_core()
    parity, has_below, has_above = slab_place()
    n = mid_own.shape[1]
    for k in range(5):
        low = pick(parity, rim_a[6 + k], rim_b[6 + k], False) if k < 2 else diag[k - 2]
        high = pick(parity, rim_a[3 + k], rim_b[3 + k], True) if k > 2 else diag[n - 1 + k]
        for side, b in enumerate((low, high)):
            a = chip[(n + 1) * side + k]
            targets[side, 0, k] = jnp.where(core == 0, a, b)
            targets[side, 1, k] = jnp.where(core == 0, b, a)
    for m in range(2):
        for side in range(2):
            for r in range(2):
                e = 2 * side + r
                base[m, e] = pick(parity, warp_a[m, r], warp_b[m, r], side == 1)
                for comp in range(3):
                    if m == 0:
                        a, b = own_a[comp, r], own_b[comp, r]
                    else:
                        a, b = rim_a[2 * comp + r], rim_b[2 * comp + r]
                    held[m, comp, e] = pick(parity, a, b, side == 1)
                    mid = mid_own if m == 0 else mid_other
                    moved[side, m, comp, r + 2 * (1 - side)] = mid[comp, (n - 2) * side + r]

    def step(j, carry):
        m, e = j // 4, j % 4
        side, r = e // 2, e % 2
        at = side + r
        v = update(
            [held[m, comp, e] for comp in range(3)], base[m, e],
            targets[side, m, at], targets[side, m, at + 1], targets[side, m, at + 2],
            jnp.where(side == 0, has_below, has_above),
        )
        for comp in range(3):
            moved[side, m, comp, e] = v[comp]
        return carry

    lax.fori_loop(0, 8, step, 0)

    def smooth(e, carry):
        side, r = e // 2, e % 2
        valid = (side == r) & jnp.where(side == 0, has_below, has_above) | (side != r)
        for comp in range(3):
            both = [blur([moved[side, m, comp, r + k] for k in range(3)]) for m in range(2)]
            for m in range(2):
                both[m] = jnp.where(valid, both[m], 0.0)
                out[m, comp, e] = both[m]
            out_sum[comp, e] = both[0] + both[1]
        return carry

    lax.fori_loop(0, 4, smooth, 0)


def second_mid_kernel(vel, beside, warp, warp_other, targets, moved, out, out_sum):
    x, _ = chip_and_core()
    inner, half = vel.shape[2], out.shape[3]

    def step(i, carry):
        for m in range(2):
            v = [(2.0 * vel[m, comp, i] + beside[comp, i]) * 0.25 for comp in range(3)]
            base = warp[i + 1] if m == 0 else warp_other[i + 1]
            v = update(v, base, targets[m, i + 1], targets[m, i + 2], targets[m, i + 3], None)
            for comp in range(3):
                moved[m, comp, i] = v[comp]
        return carry

    lax.fori_loop(0, inner, step, 0)

    def smooth(i, carry):
        for comp in range(3):
            both = [blur([moved[m, comp, i + k] for k in range(3)], (x, half)) for m in range(2)]
            for m in range(2):
                out[m, comp, i] = both[m]
            out_sum[comp, i] = both[0] + both[1]
        return carry

    lax.fori_loop(0, inner - 2, smooth, 0)


def second_rim_kernel(
    vel, beside, warp, warp_other, warp_a, warp_b, mid, targets, out, out_sum, base, moved
):
    x, _ = chip_and_core()
    parity, has_below, has_above = slab_place()
    inner, half = mid.shape[2], out.shape[3]
    n = inner + 2
    for m in range(2):
        own = warp if m == 0 else warp_other
        base[m, 0] = pick(parity, warp_a[m, 1], warp_b[m, 1], False)
        base[m, 1] = own[0]
        base[m, 2] = own[n - 1]
        base[m, 3] = pick(parity, warp_a[m, 0], warp_b[m, 0], True)
        for comp in range(3):
            for r in range(2):
                moved[0, m, comp, 2 + r] = mid[m, comp, r]
                moved[1, m, comp, r] = mid[m, comp, inner - 2 + r]

    def step(j, carry):
        m, e = j // 4, j % 4
        side, r = e // 2, e % 2
        at = 1 - side + r
        valid = (side == r) & jnp.where(side == 0, has_below, has_above) | (side != r)
        v = update(
            [(2.0 * vel[m, comp, e] + beside[comp, e]) * 0.25 for comp in range(3)], base[m, e],
            targets[side, m, at], targets[side, m, at + 1], targets[side, m, at + 2], valid,
        )
        for comp in range(3):
            moved[side, m, comp, e] = v[comp]
        return carry

    lax.fori_loop(0, 8, step, 0)

    def smooth(e, carry):
        side, r = e // 2, e % 2
        for comp in range(3):
            both = [
                blur([moved[side, m, comp, r + k] for k in range(3)], (x, half)) for m in range(2)
            ]
            for m in range(2):
                out[m, comp, e] = both[m]
            out_sum[comp, e] = both[0] + both[1]
        return carry

    lax.fori_loop(0, 4, smooth, 0)


def send_kernel(vel, beside, out):
    out[...] = (2.0 * vel[1] + beside[...]) * 0.25


def close_own_kernel(mid, mid_beside, rim, rim_beside, out, stage_mid, stage_rim, sem):
    x, _ = chip_and_core()
    half = stage_mid.shape[2]
    rows = pl.ds(pl.multiple_of(x * half, 8), half)
    n = out.shape[1]
    stage_mid[...] = (2.0 * mid[0] + mid_beside[...]) * 0.25
    stage_rim[...] = (2.0 * rim[0] + rim_beside[...]) * 0.25
    copies = [
        pltpu.make_async_copy(stage_mid, out.at[:, pl.ds(2, n - 4), rows, :], sem.at[0]),
        pltpu.make_async_copy(stage_rim.at[:, pl.ds(0, 2)], out.at[:, pl.ds(0, 2), rows, :], sem.at[1]),
        pltpu.make_async_copy(stage_rim.at[:, pl.ds(2, 2)], out.at[:, pl.ds(n - 2, 2), rows, :], sem.at[2]),
    ]
    for copy in copies:
        copy.start()
    for copy in copies:
        copy.wait()


def close_mid_kernel(done, home, out, sem):
    del done
    x, _ = chip_and_core()
    half = home.shape[2]
    rows = pl.ds(pl.multiple_of((1 - x) * half, 8), half)
    copy = pltpu.make_async_copy(home, out.at[:, pl.ds(2, out.shape[1] - 4), rows, :], sem)
    copy.start()
    copy.wait()


def close_rim_kernel(done, home, out, sem):
    del done
    x, _ = chip_and_core()
    half = home.shape[2]
    rows = pl.ds(pl.multiple_of((1 - x) * half, 8), half)
    copies = [
        pltpu.make_async_copy(
            home.at[:, pl.ds(2 * k, 2)], out.at[:, pl.ds(z, 2), rows, :], sem.at[k]
        )
        for k, z in enumerate((0, out.shape[1] - 2))
    ]
    for copy in copies:
        copy.start()
    for copy in copies:
        copy.wait()


def swaps(count, first):
    pairs = []
    for i in range(first, count - 1, 2):
        pairs += [(i, i + 1), (i + 1, i)]
    return pairs


def swap_slabs(buf_a, buf_b):
    count = lax.axis_size("slab")
    got_a = lax.ppermute(buf_a, "slab", swaps(count, 0))
    got_b = lax.ppermute(buf_b, "slab", swaps(count, 1))
    return got_a, got_b


def swap_phases(values, mask):
    return lax.ppermute(values, "phase", [(i, i ^ mask) for i in range(lax.axis_size("phase"))])


def ring_of_four(fine_images, offsets, velocity_init):
    return four_phases(fine_images, offsets, velocity_init)


def four_phases(fine_images, offsets, velocity_init):
    fine, offs, vel = fine_images[0], offsets[0], velocity_init[0]
    deep, tall, wide = fine.shape
    n, rows, cols = offs.shape[1:]
    half = rows // 2
    span = half + RIM
    lanes = 128
    dma = pltpu.SemaphoreType.DMA

    (vel_cut,) = launch(
        cut_kernel,
        [shape(3 * n * (half + 2), cols)],
        [vel],
        [pltpu.VMEM((3, n, span, cols), F32), dma],
        hbm=(0,),
        micros=1.0,
    )
    vel_far = swap_phases(vel_cut, 2)

    part, edge, buf_a, buf_b = launch(
        halve_kernel,
        [shape(n, rows, cols), shape(2, rows, cols), shape(4, rows, cols), shape(4, rows, cols)],
        [fine],
        [
            pltpu.VMEM((deep, tall, wide), F32),
            pltpu.VMEM((wide, cols), BF16),
            pltpu.VMEM((cols // lanes, 2 * tall, lanes), F32),
            pltpu.VMEM((rows, cols), F32),
            dma((n,)),
        ],
        hbm=(0,),
        micros=4.0,
    )
    got_a, got_b = swap_slabs(buf_a, buf_b)
    buf_a, buf_b = launch(
        rim_own_kernel,
        [shape(3, 2, span, cols)] * 2,
        [vel],
        [pltpu.VMEM((2, 3, 2, span, cols), F32), dma((2,))],
        hbm=(0,),
    )
    own_a, own_b = swap_slabs(buf_a, buf_b)
    ext, near, far = launch(
        join_kernel,
        [shape(n + 6, rows, cols), shape(n + 6, span, cols), shape((n + 2) * (half + 4), cols)],
        [part, edge, got_a, got_b],
    )
    chip = swap_phases(near, 1)
    diag_far = swap_phases(far, 3)

    warp, warp_cut = launch(
        warp_kernel,
        [shape(n, span, cols), shape(n * (half + 2), cols)],
        [ext, offs],
        [
            pltpu.VMEM((5, cols // lanes, n + 4, rows + 16, lanes), F32),
            pltpu.VMEM((n, rows, cols), F32),
        ],
        micros=8.5,
    )
    warp_far = swap_phases(warp_cut, 2)

    buf_a, buf_b, vel_other, diag = launch(
        rim_other_kernel,
        [shape(8, span, cols)] * 2 + [shape(3, n, span, cols), shape(n + 2, span, cols)],
        [vel_far, diag_far],
    )
    rim_a, rim_b = swap_slabs(buf_a, buf_b)
    buf_a, buf_b, warp_other = launch(
        rim_warp_kernel,
        [shape(2, 2, span, cols)] * 2 + [shape(n, span, cols)],
        [warp, warp_far],
    )
    warp_a, warp_b = swap_slabs(buf_a, buf_b)

    moved_own, targets = launch(
        first_own_kernel,
        [shape(3, n, span, cols), shape(2, n + 2, span, cols)],
        [vel, warp, chip, diag],
        micros=1.5,
    )
    moved, mid, mid_sum = launch(
        first_mid_kernel,
        [shape(3, n, span, cols), shape(2, 3, n - 2, span, cols), shape(3, n - 2, span, cols)],
        [vel_other, warp_other, moved_own, targets],
        micros=2.0,
    )
    mid_beside = swap_phases(mid_sum, 1)
    rim, rim_sum, ends = launch(
        first_rim_kernel,
        [shape(2, 3, 4, span, cols), shape(3, 4, span, cols), shape(2, 2, 5, span, cols)],
        [own_a, own_b, rim_a, rim_b, warp_a, warp_b, chip, diag, moved_own, moved],
        [
            pltpu.VMEM((2, 3, 4, span, cols), F32),
            pltpu.VMEM((2, 4, span, cols), F32),
            pltpu.VMEM((2, 2, 3, 4, span, cols), F32),
        ],
        micros=2.0,
    )
    rim_beside = swap_phases(rim_sum, 1)
    moved, mid, mid_sum = launch(
        second_mid_kernel,
        [
            shape(2, 3, n - 2, span, cols),
            shape(2, 3, n - 4, half, cols),
            shape(3, n - 4, half, cols),
        ],
        [mid, mid_beside, warp, warp_other, targets],
        micros=2.5,
    )
    mid_beside = swap_phases(mid_sum, 1)
    rim, rim_sum = launch(
        second_rim_kernel,
        [shape(2, 3, 4, half, cols), shape(3, 4, half, cols)],
        [rim, rim_beside, warp, warp_other, warp_a, warp_b, moved, ends],
        [
            pltpu.VMEM((2, 4, span, cols), F32),
            pltpu.VMEM((2, 2, 3, 4, span, cols), F32),
        ],
        micros=2.0,
    )
    rim_beside = swap_phases(rim_sum, 1)
    (away,) = launch(send_kernel, [shape(3, n - 4, half, cols)], [mid, mid_beside])
    mid_home = swap_phases(away, 2)
    (away,) = launch(send_kernel, [shape(3, 4, half, cols)], [rim, rim_beside])
    rim_home = swap_phases(away, 2)
    (velocity,) = launch(
        close_own_kernel,
        [shape(3, n, rows, cols)],
        [mid, mid_beside, rim, rim_beside],
        [
            pltpu.VMEM((3, n - 4, half, cols), F32),
            pltpu.VMEM((3, 4, half, cols), F32),
            dma((3,)),
        ],
        hbm_out=(0,),
    )
    for kernel, home, sems in ((close_mid_kernel, mid_home, dma), (close_rim_kernel, rim_home, dma((2,)))):
        (velocity,) = launch(
            kernel,
            [shape(3, n, rows, cols)],
            [velocity, home],
            [sems],
            hbm=(0,),
            hbm_out=(0,),
            alias={0: 0},
        )
    return velocity[None]


highest = lax.Precision.HIGHEST


def extended(cells, sides, width):
    for axis, dim in sides:
        count = lax.axis_size(axis)
        ends = count - 1
        head = lax.slice_in_dim(cells, 0, width, axis=dim)
        tail = lax.slice_in_dim(cells, cells.shape[dim] - width, cells.shape[dim], axis=dim)
        cells = jnp.concatenate(
            [
                lax.ppermute(tail, axis, [(i, (i + 1) % count) for i in range(ends)]),
                cells,
                lax.ppermute(head, axis, [((i + 1) % count, i) for i in range(ends)]),
            ],
            axis=dim,
        )
    return cells


def passed_along(block, axis, distance):
    devices = range(lax.axis_size(axis))
    route = [((i - distance) % len(devices), i) for i in devices]
    return lax.ppermute(block, axis, route)


def pad_axis(values, dimension, width):
    widths = [(0, 0)] * values.ndim
    widths[dimension] = (width, width)
    return jnp.pad(values, widths)


def halve_matrix(length):
    fine_index = lax.broadcasted_iota(jnp.int32, (length, length // 2), 0)
    coarse_index = lax.broadcasted_iota(jnp.int32, (length, length // 2), 1)
    outer = (fine_index == 2 * coarse_index - 1) | (fine_index == 2 * coarse_index + 2)
    inner = (fine_index == 2 * coarse_index) | (fine_index == 2 * coarse_index + 1)
    return jnp.where(inner, 0.375, jnp.where(outer, 0.125, 0.0)).astype(jnp.float32)


def smooth_matrix(length):
    source = lax.broadcasted_iota(jnp.int32, (length, length), 0)
    result = lax.broadcasted_iota(jnp.int32, (length, length), 1)
    return jnp.where(
        source == result, 0.5, jnp.where(jnp.abs(source - result) == 1, 0.25, 0.0)
    ).astype(jnp.float32)


def gradient_matrix(length):
    source = lax.broadcasted_iota(jnp.int32, (length, length), 0)
    result = lax.broadcasted_iota(jnp.int32, (length, length), 1)
    return jnp.where(source == result + 1, 0.5, jnp.where(source == result - 1, -0.5, 0.0)).astype(
        jnp.float32
    )


def along_last(values, matrix):
    return jnp.einsum("...j,jk->...k", values, matrix, precision=highest)


def along_rows(values, matrix):
    return jnp.einsum("...jx,jk->...kx", values, matrix, precision=highest)


def halve_depth(values):
    count, depth = (values.shape[0], values.shape[1])
    pairs = values.reshape((count, depth // 2, 2) + values.shape[2:])
    even = pairs[:, :, 0]
    odd = pairs[:, :, 1]
    return (even[:, :-1] + 3.0 * odd[:, :-1] + 3.0 * even[:, 1:] + odd[:, 1:]) * 0.125


def depth_gradient(values):
    length = values.shape[1] - 2
    return (values[:, 2 : 2 + length] - values[:, 0:length]) * 0.5


def depth_smooth(values):
    length = values.shape[2] - 2
    return (
        values[:, :, 0:length] + 2.0 * values[:, :, 1 : 1 + length] + values[:, :, 2 : 2 + length]
    ) * 0.25


def axis_weights(offsets):
    return [
        jnp.where(
            2 * displace == offsets, 1.0, jnp.where(jnp.abs(2 * displace - offsets) == 1, 0.5, 0.0)
        ).astype(jnp.float32)
        for displace in range(-2, 3)
    ]


def warp_moving(moving_rows, offsets):
    layers, height, breadth = (offsets.shape[2], offsets.shape[3], offsets.shape[4])
    weights_z = axis_weights(offsets[:, 0])
    weights_y = axis_weights(offsets[:, 1])
    weights_x = axis_weights(offsets[:, 2])
    shape = offsets[:, 0].shape
    rows_padded = pad_axis(moving_rows, 2, 2)
    wide = pad_axis(rows_padded, 3, 2)
    shifted = [wide[..., index_x : index_x + breadth] for index_x in range(5)]
    warped = jnp.zeros(shape, jnp.float32)
    for index_z in range(5):
        plane_sum = jnp.zeros(shape, jnp.float32)
        for index_y in range(5):
            line_sum = jnp.zeros(shape, jnp.float32)
            for index_x in range(5):
                window = shifted[index_x][:, index_z : index_z + layers, index_y : index_y + height]
                line_sum = line_sum + weights_x[index_x] * window
            plane_sum = plane_sum + weights_y[index_y] * line_sum
        warped = warped + weights_z[index_z] * plane_sum
    return warped


def shards(fine_images, offsets, velocity_init):
    fine_height, fine_breadth = (fine_images.shape[2], fine_images.shape[3])
    rimmed_fine = extended(fine_images, (("slab", 1),), 1)
    coarse = halve_depth(rimmed_fine)
    coarse = along_rows(coarse, halve_matrix(fine_height))
    coarse = along_last(coarse, halve_matrix(fine_breadth))
    target = passed_along(coarse, "phase", -1)
    height, breadth = (coarse.shape[2], coarse.shape[3])
    moving_rows = extended(coarse, (("slab", 1),), 2)
    target_rows = extended(target, (("slab", 1),), 1)
    grad_z = depth_gradient(target_rows)
    grad_y = along_rows(target, gradient_matrix(height))
    grad_x = along_last(target, gradient_matrix(breadth))
    gradients = jnp.stack([grad_z, grad_y, grad_x], axis=1)
    norm_squared = grad_z * grad_z + grad_y * grad_y + grad_x * grad_x
    warped_base = warp_moving(moving_rows, offsets)
    smooth_rows = smooth_matrix(height)
    smooth_columns = smooth_matrix(breadth)
    velocity = velocity_init
    for _ in range(ITERS):
        warped = (
            warped_base
            + velocity[:, 0] * grad_z
            + velocity[:, 1] * grad_y
            + velocity[:, 2] * grad_x
        )
        mismatch = warped - target
        denominator = norm_squared + mismatch * mismatch + 1.0
        velocity = velocity - (mismatch / denominator)[:, None] * gradients
        rimmed = extended(velocity, (("slab", 2),), 1)
        velocity = depth_smooth(rimmed)
        velocity = along_rows(velocity, smooth_rows)
        velocity = along_last(velocity, smooth_columns)
        earlier = passed_along(velocity, "phase", 1)
        later = passed_along(velocity, "phase", -1)
        velocity = (earlier + 2.0 * velocity + later) * 0.25
    return velocity


def solution(mesh):
    placed = (
        P(("case", "phase"), "slab", None, None),
        P(("case", "phase"), None, "slab", None, None),
        P(("case", "phase"), None, "slab", None, None),
    )
    four = mesh.shape["phase"] == 4
    return jax.shard_map(
        ring_of_four if four else shards,
        mesh=mesh,
        in_specs=placed,
        out_specs=P(("case", "phase"), None, "slab", None, None),
        check_vma=False,
    )
```
